32 devices in a mesh: seq: 8 (over z, x), tp: 4 (over y, core).
Axes of the slice: x: 2, y: 2, z: 4, core: 2. Of those that a mesh axis runs over, the one named last changes fastest.
Arguments:
- tokens: bfloat16 [2048, 4096], P(('seq', 'tp')), may hold values from -6 to 6
- qkv_weight: bfloat16 [4096, 1536], P(None, 'tp'), may hold values from -0.09375 to 0.09375
- out_weight: bfloat16 [512, 4096], P('tp'), may hold values from -0.25 to 0.25
- norm_gain: float32 [512], P('tp'), may hold values from 0.1 to 1.9
- doc_lengths: int32 [2], replicated, may hold values from 1 to 1536, 2048 in all
Outputs:
- layer_out: bfloat16 [2048, 4096], P(('seq', 'tp'))
The draws below stay inside these ranges and needn't reach their ends.
Inputs may be any that keep to these rules, and one draw needn't show every extreme that they name: `doc_lengths`: the lengths sum to 2048; the longest is at most 1536.
All inputs are finite; a program needn't handle non-finite values.
Results may differ from the reference program's by a relative error of at most 0.014.
Values may be sent and summed in bfloat16 or wider, within the bound.
No kernel may reach another device: no remote copies, remote signals or barrier semaphores. Data moves between devices by JAX's collectives and lax.ppermute only.
A program may use at most 64 MiB of HBM per device.

```python
import math
import jax
import jax.numpy as jnp
import numpy as np
from jax import lax

D = 4096
DH = 128
TOK_SEQ = 256
HEADS = 4
TOKENS = 2048
DOCS = 2
MOST = 1536
N_SEQ = 8


def steps_of(stream_key, dims, pieces, smallest, largest):
    level = 1.0
    for dim, shards_of in pieces:
        heights = jax.random.uniform(jax.random.fold_in(jax.random.fold_in(stream_key, 6), dim), (shards_of,), jnp.float32, smallest / len(pieces), largest / len(pieces))
        level = level * jnp.repeat(jnp.exp(heights), dims[dim] // shards_of).reshape((-1,) + (1,) * (len(dims) - 1 - dim))
    return level


def profile(number_of, total, bound, slope):
    portions = [(1 << 20) // math.isqrt(standing ** slope) + 1 for standing in range(2, number_of + 1)]
    spare, given = total - bound - (number_of - 1), [1] * (number_of - 1)
    while spare > 0:
        candidates = [i for i in range(number_of - 1) if given[i] < bound]
        mass, left = sum([portions[i] for i in candidates]), spare
        for i in candidates:
            more = min(bound - given[i], max(1, left * portions[i] // mass), spare)
            given[i] = given[i] + more
            spare = spare - more
    return np.array([bound] + given)


def uneven_parts(stream_key, amount, total, bound, skew):
    if amount == 2:
        one = jax.random.randint(stream_key, (), max(1, total - bound), min(bound, total - 1) + 1)
        return jnp.stack([one, total - one])
    sizes = jnp.asarray(profile(amount, total, bound, skew), jnp.int32)
    twos = (amount - 1) // 2
    giver, sink = sizes[1:1 + 2 * twos:2], sizes[2:2 + 2 * twos:2]
    slack = jnp.minimum(giver - 1, bound - sink)
    shifted = jax.random.randint(jax.random.fold_in(stream_key, 1), (twos,), 0, 1 << 20) % (slack + 1)
    sizes = sizes.at[1:1 + 2 * twos:2].set(giver - shifted).at[2:2 + 2 * twos:2].set(sink + shifted)
    return sizes[jax.random.permutation(jax.random.fold_in(stream_key, 2), amount)]


def normal_values(rng, shape, width, bound, cuts=(), kind=jnp.bfloat16):
    values = width * jax.random.normal(rng, shape, jnp.float32)
    if cuts:
        values = values * steps_of(rng, shape, cuts, -0.22, 0.18)
    return jnp.clip(values, -bound, bound).astype(kind)


def setup_inputs(seed: int = 0) -> dict:
    key_of = jax.random.split(jax.random.key(seed), 6)
    return {
        "tokens": normal_values(key_of[0], (TOKENS, D), 1.0, 6.0, ((0, 32),)),
        "qkv_weight": normal_values(key_of[1], (D, 3 * HEADS * DH), D ** -0.5, 0.09375, ((1, 4),)),
        "out_weight": normal_values(key_of[2], (HEADS * DH, D), (HEADS * DH) ** -0.5, 0.25, ((0, 4),)),
        "norm_gain": jnp.clip(1.0 + 0.18 * jax.random.normal(key_of[3], (HEADS * DH,), jnp.float32), 0.1, 1.9),
        "doc_lengths": uneven_parts(key_of[4], DOCS, TOKENS, MOST, 2).astype(jnp.int32),
    }


EPSILON = 1e-06

def segment_ids(doc_lengths, position):
    doc_ends = jnp.cumsum(doc_lengths).astype(jnp.int32)
    return lax.optimization_barrier(jnp.sum((doc_ends[None, :] <= position[:, None]).astype(jnp.int32), axis=1)).astype(jnp.int32)

def reference(tokens, qkv_weight, out_weight, norm_gain, doc_lengths):
    position = jnp.arange(TOKENS, dtype=jnp.int32)
    doc_ids = segment_ids(doc_lengths, position).reshape(N_SEQ, TOK_SEQ)
    causal = jnp.tril(jnp.ones((TOK_SEQ, TOK_SEQ), dtype=bool))

    def one_block(state_pair, inputs):
        carried, prior_doc = state_pair
        queries, key_rows, values, block_ids = inputs
        allowed = causal & (block_ids[:, None] == block_ids[None, :])
        raw_scores = jnp.dot(queries, key_rows.T, preferred_element_type=jnp.float32)
        scores = jnp.where(allowed, raw_scores, 0.0).astype(jnp.bfloat16)
        attended = jnp.dot(scores, values, preferred_element_type=jnp.float32)
        incoming = jnp.dot(queries.astype(jnp.float32), carried, precision=lax.Precision.HIGHEST)
        attended = attended + jnp.where((block_ids == prior_doc)[:, None], incoming, 0.0)
        last_doc = block_ids[-1]
        tail_keys = jnp.where((block_ids == last_doc)[:, None], key_rows, jnp.zeros_like(key_rows))
        tail_state = jnp.dot(tail_keys.T, values, preferred_element_type=jnp.float32)
        carried = jnp.where(last_doc == prior_doc, carried, jnp.zeros_like(carried)) + tail_state
        return ((carried, last_doc), attended)

    def one_head(running, head_index):
        columns = lax.dynamic_slice_in_dim(qkv_weight, head_index * 3 * DH, 3 * DH, 1)
        projected = jnp.dot(tokens, columns, preferred_element_type=jnp.float32).astype(jnp.bfloat16)
        queries = projected[:, :DH].reshape(N_SEQ, TOK_SEQ, DH)
        key_rows = projected[:, DH:2 * DH].reshape(N_SEQ, TOK_SEQ, DH)
        values = projected[:, 2 * DH:].reshape(N_SEQ, TOK_SEQ, DH)
        initial = (jnp.zeros((DH, DH), jnp.float32), jnp.array(-1, jnp.int32))
        _, attended = lax.scan(one_block, initial, (queries, key_rows, values, doc_ids))
        attended = attended.reshape(TOKENS, DH)
        head_gain = lax.dynamic_slice_in_dim(norm_gain, head_index * DH, DH, 0)
        inverse_rms = lax.rsqrt(lax.optimization_barrier(jnp.mean(attended * attended, axis=1, keepdims=True)) + EPSILON)
        hidden = (attended * inverse_rms * head_gain).astype(jnp.bfloat16)
        out_rows = lax.dynamic_slice_in_dim(out_weight, head_index * DH, DH, 0)
        head_term = jnp.dot(hidden, out_rows, preferred_element_type=jnp.float32).astype(jnp.bfloat16)
        return (running + head_term.astype(jnp.float32), None)
    running, _ = lax.scan(one_head, jnp.zeros((TOKENS, D), jnp.float32), jnp.arange(HEADS, dtype=jnp.int32))
    return running.astype(jnp.bfloat16)
```

```python
import functools

import jax
import jax.numpy as jnp
from jax import lax
from jax.experimental import pallas as pl
from jax.experimental.pallas import tpu as pltpu
from jax.sharding import PartitionSpec as P

EPSILON = 1e-06
MOST = 1536

VMEM = pl.BlockSpec(memory_space=pltpu.VMEM)
SMEM = pl.BlockSpec(memory_space=pltpu.SMEM)


def doc_of(lengths_ref, position):
    end = jnp.int32(0)
    found = jnp.zeros_like(position)
    for d in range(lengths_ref.shape[0]):
        end = end + lengths_ref[d]
        found = found + (position >= end).astype(jnp.int32)
    return found


def positions(groups, rows, total, axis):
    start = lax.axis_index("seq") * total
    me = lax.axis_index("tp")
    shape = (rows, 1) if axis == 0 else (1, rows)
    row = lax.broadcasted_iota(jnp.int32, shape, axis)
    parts = [
        row + start + (jnp.bitwise_xor(me, j) * rows if groups > 1 else 0) for j in range(groups)
    ]
    return jnp.concatenate(parts, axis=axis) if groups > 1 else parts[0]


def tail_kernel(groups, lengths_ref, *refs):
    parts, out_ref = refs[:groups], refs[groups]
    rows, head = parts[0].shape[0], parts[0].shape[1] // 3
    total = groups * rows
    keys = jnp.concatenate([r[:, head : 2 * head] for r in parts], axis=0)
    values = jnp.concatenate([r[:, 2 * head :] for r in parts], axis=0)
    last = (lax.axis_index("seq") + 1) * total - 1
    same = doc_of(lengths_ref, positions(groups, rows, total, 0)) == doc_of(lengths_ref, last)
    keys = jnp.where(same, keys, jnp.zeros_like(keys))
    out_ref[...] = lax.dot_general(
        keys, values, (((0,), (0,)), ((), ())), preferred_element_type=jnp.float32
    ).astype(out_ref.dtype)


def local_kernel(groups, lengths_ref, *refs):
    parts, out_ref = refs[:groups], refs[groups]
    rows, head = parts[0].shape[0], parts[0].shape[1] // 3
    total = groups * rows
    queries = jnp.concatenate([r[:, :head] for r in parts], axis=0)
    keys = jnp.concatenate([r[:, head : 2 * head] for r in parts], axis=0)
    values = jnp.concatenate([r[:, 2 * head :] for r in parts], axis=0)
    to, of = positions(groups, rows, total, 0), positions(groups, rows, total, 1)
    allowed = (of <= to) & (doc_of(lengths_ref, of) == doc_of(lengths_ref, to))
    scores = lax.dot_general(
        queries, keys, (((1,), (1,)), ((), ())), preferred_element_type=jnp.float32
    )
    scores = jnp.where(allowed, scores, 0.0).astype(jnp.bfloat16)
    out_ref[...] = jnp.dot(scores, values, preferred_element_type=jnp.float32)


def pair_kernel(total, lengths_ref, own_ref, other_ref, out_ref):
    index = lax.axis_index("seq")
    odd = lax.rem(index, 2) == 1
    first = index - lax.rem(index, 2)
    joined = doc_of(lengths_ref, (first + 1) * total - 1) == doc_of(
        lengths_ref, (first + 2) * total - 1
    )
    own, other = own_ref[...].astype(jnp.float32), other_ref[...].astype(jnp.float32)
    low = jnp.where(odd, other, own)
    high = jnp.where(odd, own, other)
    out_ref[...] = (high + jnp.where(joined, low, 0.0)).astype(out_ref.dtype)


def finish_kernel(groups, hops, lengths_ref, *refs):
    parts, refs = refs[:groups], refs[groups:]
    local_ref, other_ref, pair_refs, gain_ref = refs[0], refs[1], refs[2 : 2 + hops], refs[2 + hops]
    outs = refs[3 + hops :]
    rows, head = parts[0].shape[0], parts[0].shape[1] // 3
    total = groups * rows
    index = lax.axis_index("seq")
    odd = lax.rem(index, 2) == 1
    first_doc = doc_of(lengths_ref, index * total)

    def reaches(last):
        return (last >= 0) & (doc_of(lengths_ref, last) == first_doc)

    state = jnp.where(
        odd & reaches(index * total - 1), other_ref[...].astype(jnp.float32), 0.0
    )
    pair = index - lax.rem(index, 2)
    for k in range(hops):
        state = state + jnp.where(
            reaches((pair - 2 * k) * total - 1), pair_refs[k][...].astype(jnp.float32), 0.0
        )
    high = state.astype(jnp.bfloat16)
    low = (state - high.astype(jnp.float32)).astype(jnp.bfloat16)
    queries = jnp.concatenate([r[:, :head] for r in parts], axis=0)
    incoming = jnp.dot(queries, high, preferred_element_type=jnp.float32) + jnp.dot(
        queries, low, preferred_element_type=jnp.float32
    )
    takes = doc_of(lengths_ref, positions(groups, rows, total, 0)) == first_doc
    attended = local_ref[...] + jnp.where(takes, incoming, 0.0)
    inverse_rms = lax.rsqrt(jnp.mean(attended * attended, axis=1, keepdims=True) + EPSILON)
    hidden = (attended * inverse_rms * gain_ref[...]).astype(jnp.bfloat16)
    for j in range(groups):
        outs[j][...] = hidden[j * rows : (j + 1) * rows]


def out_kernel(groups, *refs):
    hidden, weights, out_ref = refs[:groups], refs[groups : 2 * groups], refs[2 * groups]
    total = jnp.dot(hidden[0][...], weights[0][...], preferred_element_type=jnp.float32)
    for j in range(1, groups):
        total += jnp.dot(hidden[j][...], weights[j][...], preferred_element_type=jnp.float32)
    out_ref[...] = total.astype(out_ref.dtype)


def call(kernel, out_shape, flops, *args):
    nbytes = sum(a.size * a.dtype.itemsize for a in args)
    multiple = isinstance(out_shape, (list, tuple))
    return pl.pallas_call(
        kernel,
        out_shape=out_shape,
        in_specs=[SMEM] + [VMEM] * (len(args) - 1),
        out_specs=[VMEM] * len(out_shape) if multiple else VMEM,
        cost_estimate=pl.CostEstimate(flops=flops, bytes_accessed=nbytes, transcendentals=0),
        compiler_params=pltpu.CompilerParams(vmem_limit_bytes=4 << 20),
    )(*args)


def swap(x, axis, bits):
    return lax.ppermute(x, axis, [(i, i ^ bits) for i in range(lax.axis_size(axis))])


def body(tokens, qkv_weight, out_weight, norm_gain, doc_lengths):
    tp, seq = lax.axis_size("tp"), lax.axis_size("seq")
    head = qkv_weight.shape[1] // 3
    total = tokens.shape[0] * tp
    bf16, f32 = jnp.bfloat16, jnp.float32
    split = tp == 4
    if split:
        across = swap(tokens, "tp", 2)
        gathered = [tokens, swap(tokens, "tp", 1), across, swap(across, "tp", 1)]
        out_weight_late, _ = lax.optimization_barrier((out_weight, across))
        weight_across = swap(out_weight_late, "tp", 2)
    else:
        gathered = [lax.all_gather(tokens, "tp", axis=0, tiled=True)]
    groups = len(gathered)
    rows = gathered[0].shape[0]
    parts = [jnp.dot(x, qkv_weight, preferred_element_type=f32).astype(bf16) for x in gathered]

    square = jax.ShapeDtypeStruct((head, head), bf16)
    state_flops = 2 * total * head * head
    tail = call(functools.partial(tail_kernel, groups), square, state_flops, doc_lengths, *parts)
    other = swap(tail, "seq", 1)
    local = call(
        functools.partial(local_kernel, groups),
        jax.ShapeDtypeStruct((total, head), f32),
        4 * total * total * head,
        doc_lengths,
        *parts,
    )
    pair = call(functools.partial(pair_kernel, total), square, head * head, doc_lengths, tail, other)
    reach = -(-(MOST - 1) // total)
    hops = min(seq // 2 - 1, -(-reach // 2))
    pairs = [
        lax.ppermute(pair, "seq", [(i, (i + 2 * k) % seq) for i in range(seq)])
        for k in range(1, hops + 1)
    ]
    if split:
        weight_across, *pairs = lax.optimization_barrier((weight_across, *pairs))
        weights = [out_weight, swap(out_weight_late, "tp", 1), weight_across, swap(weight_across, "tp", 1)]
    else:
        weights = [lax.all_gather(out_weight, "tp", axis=0, tiled=True)]
    hidden = call(
        functools.partial(finish_kernel, groups, hops),
        [jax.ShapeDtypeStruct((rows, head), bf16)] * groups,
        2 * state_flops,
        doc_lengths,
        *parts,
        local,
        other,
        *pairs,
        norm_gain.reshape(1, head),
    )
    if split:
        hidden = [hidden[0]] + [swap(hidden[j], "tp", j) for j in range(1, groups)]
    else:
        mixed = lax.all_to_all(hidden[0].reshape(tp, -1, head), "tp", 0, 0, tiled=True)
        hidden = [mixed.transpose(1, 0, 2).reshape(-1, tp * head)]
    width = out_weight.shape[1]
    tile = 1024
    mine = hidden[0].shape[0]
    return pl.pallas_call(
        functools.partial(out_kernel, groups),
        out_shape=jax.ShapeDtypeStruct((mine, width), bf16),
        grid=(width // tile,),
        in_specs=[pl.BlockSpec(h.shape, lambda i: (0, 0)) for h in hidden]
        + [pl.BlockSpec((w.shape[0], tile), lambda i: (0, i)) for w in weights],
        out_specs=pl.BlockSpec((mine, tile), lambda i: (0, i)),
        compiler_params=pltpu.CompilerParams(vmem_limit_bytes=16 << 20),
    )(*hidden, *weights)


def solution(mesh):
    in_specs = (P(("seq", "tp"), None), P(None, "tp"), P("tp", None), P("tp"), P())
    out_specs = P(("seq", "tp"), None)
    return jax.shard_map(body, mesh=mesh, in_specs=in_specs, out_specs=out_specs, check_vma=False)
```

```python
import functools

import jax
import jax.numpy as jnp
from jax import lax
from jax.experimental import pallas as pl
from jax.experimental.pallas import tpu as pltpu
from jax.sharding import PartitionSpec as P

EPSILON = 1e-06
MOST = 1536

VMEM = pl.BlockSpec(memory_space=pltpu.VMEM)
SMEM = pl.BlockSpec(memory_space=pltpu.SMEM)


def doc_of(lengths_ref, position):
    end = jnp.int32(0)
    found = jnp.zeros_like(position)
    for d in range(lengths_ref.shape[0]):
        end = end + lengths_ref[d]
        found = found + (position >= end).astype(jnp.int32)
    return found


def positions(groups, rows, total, axis):
    start = lax.axis_index("seq") * total
    me = lax.axis_index("tp")
    shape = (rows, 1) if axis == 0 else (1, rows)
    row = lax.broadcasted_iota(jnp.int32, shape, axis)
    parts = [
        row + start + (jnp.bitwise_xor(me, j) * rows if groups > 1 else 0) for j in range(groups)
    ]
    return jnp.concatenate(parts, axis=axis) if groups > 1 else parts[0]


def tail_kernel(groups, late, lengths_ref, weight_ref, *refs):
    parts, fresh, (kv_ref, out_ref) = refs[: groups - late], refs[groups - late : groups], refs[groups:]
    rows, head = fresh[0].shape[0], weight_ref.shape[1] // 3
    total = groups * rows
    fresh = jnp.concatenate([r[...] for r in fresh], axis=0)
    fresh = jnp.dot(fresh, weight_ref[:, head:], preferred_element_type=jnp.float32).astype(jnp.bfloat16)
    kv_ref[...] = fresh
    keys = jnp.concatenate([r[:, head : 2 * head] for r in parts] + [fresh[:, :head]], axis=0)
    values = jnp.concatenate([r[:, 2 * head :] for r in parts] + [fresh[:, head:]], axis=0)
    last = (lax.axis_index("seq") + 1) * total - 1
    same = doc_of(lengths_ref, positions(groups, rows, total, 0)) == doc_of(lengths_ref, last)
    keys = jnp.where(same, keys, jnp.zeros_like(keys))
    out_ref[...] = lax.dot_general(
        keys, values, (((0,), (0,)), ((), ())), preferred_element_type=jnp.float32
    ).astype(out_ref.dtype)


def local_kernel(groups, late, lengths_ref, weight_ref, kv_ref, *refs):
    parts, fresh, (query_ref, out_ref) = refs[: groups - late], refs[groups - late : groups], refs[groups:]
    rows, head = fresh[0].shape[0], weight_ref.shape[1] // 3
    total = groups * rows
    fresh = jnp.concatenate([r[...] for r in fresh], axis=0)
    fresh = jnp.dot(fresh, weight_ref[:, :head], preferred_element_type=jnp.float32).astype(jnp.bfloat16)
    queries = jnp.concatenate([r[:, :head] for r in parts] + [fresh], axis=0)
    query_ref[...] = queries
    keys = jnp.concatenate([r[:, head : 2 * head] for r in parts] + [kv_ref[:, :head]], axis=0)
    values = jnp.concatenate([r[:, 2 * head :] for r in parts] + [kv_ref[:, head:]], axis=0)
    to, of = positions(groups, rows, total, 0), positions(groups, rows, total, 1)
    allowed = (of <= to) & (doc_of(lengths_ref, of) == doc_of(lengths_ref, to))
    scores = lax.dot_general(
        queries, keys, (((1,), (1,)), ((), ())), preferred_element_type=jnp.float32
    )
    scores = jnp.where(allowed, scores, 0.0).astype(jnp.bfloat16)
    out_ref[...] = jnp.dot(scores, values, preferred_element_type=jnp.float32)


def pair_kernel(total, lengths_ref, own_ref, other_ref, out_ref):
    index = lax.axis_index("seq")
    odd = lax.rem(index, 2) == 1
    first = index - lax.rem(index, 2)
    joined = doc_of(lengths_ref, (first + 1) * total - 1) == doc_of(
        lengths_ref, (first + 2) * total - 1
    )
    own, other = own_ref[...].astype(jnp.float32), other_ref[...].astype(jnp.float32)
    low = jnp.where(odd, other, own)
    high = jnp.where(odd, own, other)
    out_ref[...] = (high + jnp.where(joined, low, 0.0)).astype(out_ref.dtype)


def finish_kernel(groups, source, lengths_ref, query_ref, local_ref, other_ref, *refs):
    split = [ref.shape[0] for ref in refs].index(1)
    pair_refs, gain_ref, outs = refs[:split], refs[split], refs[split + 1 :]
    total = query_ref.shape[0]
    rows = total // groups
    index = lax.axis_index("seq")
    odd = lax.rem(index, 2) == 1
    first_doc = doc_of(lengths_ref, index * total)

    def reaches(last):
        return (last >= 0) & (doc_of(lengths_ref, last) == first_doc)

    state = jnp.where(
        odd & reaches(index * total - 1), other_ref[...].astype(jnp.float32), 0.0
    )
    pair = lax.div(index, 2)
    for k, ref in enumerate(pair_refs):
        sender = source(pair, k + 1)
        state = state + jnp.where(
            (sender < pair) & reaches((sender + 1) * 2 * total - 1), ref[...].astype(jnp.float32), 0.0
        )
    high = state.astype(jnp.bfloat16)
    low = (state - high.astype(jnp.float32)).astype(jnp.bfloat16)
    queries = query_ref[...]
    incoming = jnp.dot(queries, high, preferred_element_type=jnp.float32) + jnp.dot(
        queries, low, preferred_element_type=jnp.float32
    )
    takes = doc_of(lengths_ref, positions(groups, rows, total, 0)) == first_doc
    attended = local_ref[...] + jnp.where(takes, incoming, 0.0)
    inverse_rms = lax.rsqrt(jnp.mean(attended * attended, axis=1, keepdims=True) + EPSILON)
    hidden = (attended * inverse_rms * gain_ref[...]).astype(jnp.bfloat16)
    each = total // len(outs)
    for j, out_ref in enumerate(outs):
        out_ref[...] = hidden[j * each : (j + 1) * each]


def project_kernel(rows_ref, weight_ref, out_ref):
    out_ref[...] = jnp.dot(
        rows_ref[...], weight_ref[...], preferred_element_type=jnp.float32
    ).astype(out_ref.dtype)


def cut_kernel(weight_ref, shared_ref, rest_ref):
    share = shared_ref.shape[1]
    start = pl.multiple_of(lax.rem(lax.axis_index("seq"), 2) * share, share)
    shared_ref[...] = weight_ref[:, pl.ds(start, share)]
    rest_ref[...] = weight_ref[:, 2 * share :]


def chip_kernel(span, near_ref, far_ref, near_weight_ref, *refs):
    weights, (own_ref, other_ref) = refs[:-2], refs[-2:]
    rows = own_ref.shape[0]
    hidden = jnp.concatenate([near_ref[...], far_ref[...]], axis=1)
    mine = lax.rem(lax.axis_index("seq"), 2)
    share = weights[0].shape[1]
    starts = [mine * share, (1 - mine) * share] if span == 0 else [0]
    for start, weight_ref in zip(starts, weights):
        here = pl.ds(pl.multiple_of(start, share), share) if span == 0 else slice(None)
        columns = here if span == 0 else slice(near_weight_ref.shape[1] - share, None)
        weight = jnp.concatenate([near_weight_ref[:, columns], weight_ref[...]], axis=0)
        result = jnp.dot(hidden, weight, preferred_element_type=jnp.float32)
        own_ref[:, here] = result[:rows]
        other_ref[:, here] = result[rows:].astype(other_ref.dtype)


def sum_kernel(*refs):
    out_ref = refs[-1]
    done = 0
    for own_ref, other_ref in zip(refs[:-1:2], refs[1:-1:2]):
        width = own_ref.shape[1]
        out_ref[:, done : done + width] = (
            own_ref[...] + other_ref[...].astype(jnp.float32)
        ).astype(out_ref.dtype)
        done += width


def out_kernel(hidden_ref, weight_ref, out_ref):
    out_ref[...] = jnp.dot(
        hidden_ref[...], weight_ref[...], preferred_element_type=jnp.float32
    ).astype(out_ref.dtype)


def call(kernel, out_shape, flops, *args, scalars=True, limit=4):
    nbytes = sum(a.size * a.dtype.itemsize for a in args)
    multiple = isinstance(out_shape, (list, tuple))
    return pl.pallas_call(
        kernel,
        out_shape=out_shape,
        in_specs=[SMEM if scalars and i == 0 else VMEM for i in range(len(args))],
        out_specs=[VMEM] * len(out_shape) if multiple else VMEM,
        cost_estimate=pl.CostEstimate(flops=flops, bytes_accessed=nbytes, transcendentals=0),
        compiler_params=pltpu.CompilerParams(vmem_limit_bytes=limit << 20),
    )(*args)


def swap(x, axis, bits):
    return lax.ppermute(x, axis, [(i, i ^ bits) for i in range(lax.axis_size(axis))])


def after(x, *others):
    return lax.optimization_barrier((x, *others))[0]


def body(tokens, qkv_weight, out_weight, norm_gain, doc_lengths):
    tp, seq = lax.axis_size("tp"), lax.axis_size("seq")
    head = qkv_weight.shape[1] // 3
    mine, width = tokens.shape[0], out_weight.shape[1]
    total = mine * tp
    bf16, f32 = jnp.bfloat16, jnp.float32
    shape = jax.ShapeDtypeStruct
    split = tp == 4
    share = width // 4

    def project(x):
        return call(
            project_kernel,
            shape((x.shape[0], 3 * head), bf16),
            2 * x.size * 3 * head,
            x,
            qkv_weight,
            scalars=False,
        )

    if split:
        across = swap(tokens, "tp", 2)
        own = project(tokens)
        shared, rest = call(
            cut_kernel,
            [shape((head, share), bf16), shape((head, width - 2 * share), bf16)],
            head * width,
            out_weight,
            scalars=False,
        )
        beside = project(swap(tokens, "tp", 1))
        across, own, beside, shared, rest = lax.optimization_barrier(
            (across, own, beside, shared, rest)
        )
        parts = [own, beside, project(across)]
        late = [swap(across, "tp", 1)]
        shared = swap(shared, "tp", 2)
    else:
        parts, late = [], [lax.all_gather(tokens, "tp", axis=0, tiled=True)]
    groups = len(parts) + len(late)
    fresh = sum(x.shape[0] for x in late)
    state_flops = 2 * total * head * head
    late_kv, tail = call(
        functools.partial(tail_kernel, groups, len(late)),
        [shape((fresh, 2 * head), bf16), shape((head, head), bf16)],
        state_flops + 4 * fresh * tokens.shape[1] * head,
        doc_lengths,
        qkv_weight,
        *parts,
        *late,
    )
    other = swap(tail, "seq", 1)
    queries, local = call(
        functools.partial(local_kernel, groups, len(late)),
        [shape((total, head), bf16), shape((total, head), f32)],
        4 * total * total * head + 2 * fresh * tokens.shape[1] * head,
        doc_lengths,
        qkv_weight,
        late_kv,
        *parts,
        *late,
    )
    other = after(other, local)
    pair = call(
        functools.partial(pair_kernel, total),
        shape((head, head), bf16),
        1000000000,
        doc_lengths,
        tail,
        other,
    )
    reach = -(-(MOST - 1) // total)
    hops = min(seq // 2 - 1, -(-reach // 2))
    if seq == 8 and hops == 3:
        pairs = [swap(pair, "seq", 2 * k) for k in range(1, hops + 1)]
        source = jnp.bitwise_xor
    else:
        pairs = [
            lax.ppermute(pair, "seq", [(i, (i + 2 * k) % seq) for i in range(seq)])
            for k in range(1, hops + 1)
        ]
        source = jnp.subtract
    if split:
        rest = swap(after(rest, local), "tp", 2)
        shared_other = swap(after(shared, pair), "seq", 1)
    hidden = call(
        functools.partial(finish_kernel, groups, source),
        [shape((total // 2, head), bf16)] * 2 if split else [shape((total, head), bf16)],
        4250000000,
        doc_lengths,
        queries,
        local,
        other,
        *pairs,
        norm_gain.reshape(1, head),
    )
    out = shape((mine, width), bf16)
    if not split:
        mixed = lax.all_to_all(hidden[0].reshape(tp, -1, head), "tp", 0, 0, tiled=True)
        mixed = mixed.transpose(1, 0, 2).reshape(-1, tp * head)
        weight = lax.all_gather(out_weight, "tp", axis=0, tiled=True)
        tile = width // 4
        return pl.pallas_call(
            out_kernel,
            out_shape=out,
            grid=(width // tile,),
            in_specs=[
                pl.BlockSpec(mixed.shape, lambda i: (0, 0)),
                pl.BlockSpec((weight.shape[0], tile), lambda i: (0, i)),
            ],
            out_specs=pl.BlockSpec((mine, tile), lambda i: (0, i)),
        )(mixed, weight)
    near, far = hidden
    far = swap(far, "tp", 2)
    shared, shared_other, rest = lax.optimization_barrier((shared, shared_other, rest))
    sums = []
    for span, pieces in enumerate([[shared, shared_other], [rest]]):
        columns = sum(w.shape[1] for w in pieces)
        own, other = call(
            functools.partial(chip_kernel, span),
            [shape((mine, columns), f32), shape((mine, columns), bf16)],
            8 * mine * head * columns,
            near,
            far,
            out_weight,
            *pieces,
            scalars=False,
        )
        sums += [own, swap(other, "tp", 1)]
    return call(sum_kernel, out, mine * width, *sums, scalars=False)


def solution(mesh):
    in_specs = (P(("seq", "tp"), None), P(None, "tp"), P("tp", None), P("tp"), P())
    out_specs = P(("seq", "tp"), None)
    return jax.shard_map(body, mesh=mesh, in_specs=in_specs, out_specs=out_specs, check_vma=False)
```

```python
import functools

import jax
import jax.numpy as jnp
from jax import lax
from jax.experimental import pallas as pl
from jax.experimental.pallas import tpu as pltpu
from jax.sharding import PartitionSpec as P

EPSILON = 1e-06
MOST = 1536

VMEM = pl.BlockSpec(memory_space=pltpu.VMEM)
SMEM = pl.BlockSpec(memory_space=pltpu.SMEM)


def doc_of(lengths_ref, position):
    end = jnp.int32(0)
    found = jnp.zeros_like(position)
    for d in range(lengths_ref.shape[0]):
        end = end + lengths_ref[d]
        found = found + (position >= end).astype(jnp.int32)
    return found


def mask_kernel(hops, source, lengths_ref, *refs):
    keep_refs, takes_ref, allowed_ref, flags_ref = refs[:-3], refs[-3], refs[-2], refs[-1]
    groups, (rows, lanes) = len(keep_refs), keep_refs[0].shape
    total = groups * rows
    index, me = lax.axis_index("seq"), lax.axis_index("tp")
    odd = lax.rem(index, 2) == 1
    first_doc = doc_of(lengths_ref, index * total)
    last_doc = doc_of(lengths_ref, (index + 1) * total - 1)

    def positions(shape, axis):
        row = lax.broadcasted_iota(jnp.int32, shape, axis)
        found = row + index * total
        if groups > 1:
            group = lax.div(row, rows)
            for j in range(groups):
                shift = (jnp.bitwise_xor(me, j) - j) * rows
                found = found + jnp.where(group == j, shift, 0)
        return found

    doc = doc_of(lengths_ref, positions((total, lanes), 0))
    takes_ref[...] = (doc == first_doc).astype(jnp.float32)
    keep = (doc == last_doc).astype(jnp.float32).astype(jnp.bfloat16)
    for j, ref in enumerate(keep_refs):
        ref[...] = keep[j * rows : (j + 1) * rows]
    to, of = positions((total, total), 0), positions((total, total), 1)
    allowed = (of <= to) & (doc_of(lengths_ref, of) == doc_of(lengths_ref, to))
    allowed_ref[...] = allowed.astype(jnp.float32).astype(jnp.bfloat16)

    def reaches(last, doc):
        return (last >= 0) & (doc_of(lengths_ref, last) == doc)

    pair = lax.div(index, 2)
    joined = reaches((2 * pair + 1) * total - 1, doc_of(lengths_ref, (2 * pair + 2) * total - 1))
    flags = [odd | joined, jnp.logical_not(odd) | joined, odd & reaches(index * total - 1, first_doc)]
    for k in range(1, hops + 1):
        sender = source(pair, k)
        flags.append((sender < pair) & reaches((sender + 1) * 2 * total - 1, first_doc))
    row = lax.broadcasted_iota(jnp.int32, flags_ref.shape, 0)
    found = jnp.zeros(flags_ref.shape, jnp.int32)
    for i, flag in enumerate(flags):
        found = found + jnp.where(row == i, flag.astype(jnp.int32), 0)
    flags_ref[...] = found.astype(jnp.float32)


def project_kernel(before, first, rows_ref, weight_ref, keep_ref, *refs):
    out_ref, state_ref = refs[before:]
    head = keep_ref.shape[1]
    found = jnp.dot(
        rows_ref[...], weight_ref[:, first:], preferred_element_type=jnp.float32
    ).astype(jnp.bfloat16)
    out_ref[...] = found
    keys, values = found[:, -2 * head : -head] * keep_ref[...], found[:, -head:]
    state = lax.dot_general(
        keys, values, (((0,), (0,)), ((), ())), preferred_element_type=jnp.float32
    )
    if before:
        state = state + refs[0][...]
    state_ref[...] = state.astype(state_ref.dtype)


def local_kernel(late_ref, weight_ref, late_kv_ref, allowed_ref, *refs):
    parts, query_ref, out_ref = refs[:-2], refs[-2], refs[-1]
    head = weight_ref.shape[1] // 3
    late = jnp.dot(
        late_ref[...], weight_ref[:, :head], preferred_element_type=jnp.float32
    ).astype(jnp.bfloat16)
    queries = jnp.concatenate([r[:, :head] for r in parts] + [late], axis=0)
    query_ref[...] = queries
    keys = jnp.concatenate([r[:, head : 2 * head] for r in parts] + [late_kv_ref[:, :head]], axis=0)
    values = jnp.concatenate([r[:, 2 * head :] for r in parts] + [late_kv_ref[:, head:]], axis=0)
    scores = lax.dot_general(
        queries, keys, (((1,), (1,)), ((), ())), preferred_element_type=jnp.float32
    )
    scores = scores.astype(jnp.bfloat16) * allowed_ref[...]
    out_ref[...] = jnp.dot(scores, values, preferred_element_type=jnp.float32)


def pair_kernel(flags_ref, own_ref, other_ref, out_ref):
    out_ref[...] = (
        own_ref[...].astype(jnp.float32) * flags_ref[0:1, :]
        + other_ref[...].astype(jnp.float32) * flags_ref[1:2, :]
    ).astype(out_ref.dtype)


def finish_kernel(hops, flags_ref, query_ref, local_ref, takes_ref, gain_ref, *refs):
    state_refs, outs = refs[: hops + 1], refs[hops + 1 :]
    state = jnp.zeros(state_refs[0].shape, jnp.float32)
    for k, ref in enumerate(state_refs):
        state = state + ref[...].astype(jnp.float32) * flags_ref[2 + k : 3 + k, :]
    high = state.astype(jnp.bfloat16)
    low = (state - high.astype(jnp.float32)).astype(jnp.bfloat16)
    queries = query_ref[...]
    incoming = jnp.dot(queries, high, preferred_element_type=jnp.float32) + jnp.dot(
        queries, low, preferred_element_type=jnp.float32
    )
    attended = local_ref[...] + incoming * takes_ref[...]
    inverse_rms = lax.rsqrt(jnp.mean(attended * attended, axis=1, keepdims=True) + EPSILON)
    hidden = (attended * inverse_rms * gain_ref[...]).astype(jnp.bfloat16)
    each = hidden.shape[0] // len(outs)
    for j, out_ref in enumerate(outs):
        out_ref[...] = hidden[j * each : (j + 1) * each]


def piece_at(bits, width):
    place = jnp.bitwise_xor(lax.rem(lax.axis_index("seq"), 4), bits)
    return pl.ds(pl.multiple_of(place * width, 128), width)


def cut_kernel(weight_ref, shared_ref, rest_ref):
    piece = shared_ref.shape[1]
    shared_ref[...] = weight_ref[:, piece_at(0, piece)]
    rest_ref[:, :piece] = weight_ref[:, piece_at(3, piece)]
    rest_ref[:, piece:] = weight_ref[:, 4 * piece :]


def chip_kernel(places, piece, near_ref, far_ref, near_weight_ref, *refs):
    weights, (own_ref, other_ref) = refs[:-2], refs[-2:]
    rows = own_ref.shape[0]
    hidden = jnp.concatenate([near_ref[...], far_ref[...]], axis=1)
    done = 0
    for place, weight_ref in zip(places, weights):
        width = weight_ref.shape[1]
        near = near_weight_ref[:, piece_at(place, piece)]
        if width > piece:
            near = jnp.concatenate([near, near_weight_ref[:, 4 * piece :]], axis=1)
        weight = jnp.concatenate([near, weight_ref[...]], axis=0)
        result = jnp.dot(hidden, weight, preferred_element_type=jnp.float32)
        own_ref[:, done : done + width] = result[:rows]
        other_ref[:, done : done + width] = result[rows:].astype(other_ref.dtype)
        done += width


def sum_kernel(places, piece, *refs):
    out_ref = refs[-1]
    for each, own_ref, other_ref in zip(places, refs[:-1:2], refs[1:-1:2]):
        for k, place in enumerate(each):
            here = slice(k * piece, (k + 1) * piece)
            out_ref[:, piece_at(place, piece)] = (
                own_ref[:, here] + other_ref[:, here].astype(jnp.float32)
            ).astype(out_ref.dtype)
        if own_ref.shape[1] > len(each) * piece:
            out_ref[:, 4 * piece :] = (
                own_ref[:, len(each) * piece :]
                + other_ref[:, len(each) * piece :].astype(jnp.float32)
            ).astype(out_ref.dtype)


def out_kernel(hidden_ref, weight_ref, out_ref):
    out_ref[...] = jnp.dot(
        hidden_ref[...], weight_ref[...], preferred_element_type=jnp.float32
    ).astype(out_ref.dtype)


def call(kernel, out_shape, flops, *args, scalars=False):
    several = isinstance(out_shape, (list, tuple))
    return pl.pallas_call(
        kernel,
        out_shape=out_shape,
        in_specs=[SMEM if scalars and i == 0 else VMEM for i in range(len(args))],
        out_specs=[VMEM] * len(out_shape) if several else VMEM,
        cost_estimate=pl.CostEstimate(
            flops=flops,
            bytes_accessed=sum(a.size * a.dtype.itemsize for a in args) if flops else 0,
            transcendentals=0,
        ),
        compiler_params=pltpu.CompilerParams(vmem_limit_bytes=4 << 20),
    )(*args)


def swap(x, axis, bits):
    return lax.ppermute(x, axis, [(i, i ^ bits) for i in range(lax.axis_size(axis))])


def after(x, *others):
    return lax.optimization_barrier((x, *others))[0]


def body(tokens, qkv_weight, out_weight, norm_gain, doc_lengths):
    tp, seq = lax.axis_size("tp"), lax.axis_size("seq")
    head = qkv_weight.shape[1] // 3
    mine, width = tokens.shape[0], out_weight.shape[1]
    total = mine * tp
    bf16, f32 = jnp.bfloat16, jnp.float32
    shape = jax.ShapeDtypeStruct
    square = shape((head, head), bf16)
    split = tp == 4 and seq % 4 == 0
    groups = 4 if split else 1
    rows = total // groups
    piece = 7 * width // 32

    reach = -(-(MOST - 1) // total)
    hops = min(seq // 2 - 1, -(-reach // 2))
    everyone = seq == 8 and hops == 3
    *keep, takes, allowed, flags = call(
        functools.partial(mask_kernel, hops, jnp.bitwise_xor if everyone else jnp.subtract),
        [shape((rows, head), bf16)] * groups
        + [shape((total, head), f32), shape((total, total), bf16), shape((8, head), f32)],
        total * total,
        doc_lengths,
        scalars=True,
    )

    def project(x, group, *before, first=0, state_type=f32, cost=None):
        return call(
            functools.partial(project_kernel, len(before), first),
            [shape((rows, 3 * head - first), bf16), shape((head, head), state_type)],
            6 * x.size * head if cost is None else cost,
            x,
            qkv_weight,
            keep[group],
            *before,
        )

    if split:
        across = swap(tokens, "tp", 2)
        own, state = project(tokens, 0)
        beside, state = project(swap(tokens, "tp", 1), 1, state, cost=0)
        shared, rest = call(
            cut_kernel,
            [shape((head, piece), bf16), shape((head, width - 3 * piece), bf16)],
            head * width,
            out_weight,
        )
        across, own, beside, state, shared, rest, takes, allowed, flags, *keep = (
            lax.optimization_barrier(
                (across, own, beside, state, shared, rest, takes, allowed, flags, *keep)
            )
        )
        late = swap(across, "tp", 1)
        shared = swap(shared, "tp", 2)
        part, state = project(across, 2, state)
        parts, before = [own, beside, part], [state]
    else:
        late = lax.all_gather(tokens, "tp", axis=0, tiled=True)
        parts, before = [], []
    late_kv, tail = project(late, groups - 1, *before, first=head, state_type=bf16)
    other = swap(tail, "seq", 1)
    queries, local = call(
        local_kernel,
        [shape((total, head), bf16), shape((total, head), f32)],
        4 * total * total * head + 2 * late.size * head,
        late,
        qkv_weight,
        late_kv,
        allowed,
        *parts,
    )
    other = after(other, local)
    pair = call(pair_kernel, square, 1000000000, flags, tail, other)
    if everyone:
        pairs = [swap(pair, "seq", 2 * k) for k in range(1, hops + 1)]
    else:
        pairs = [
            lax.ppermute(pair, "seq", [(i, (i + 2 * k) % seq) for i in range(seq)])
            for k in range(1, hops + 1)
        ]
    if split:
        rest = swap(after(rest, local), "tp", 2)
        shared = after(shared, pair)
        shared_x, shared_z = swap(shared, "seq", 1), swap(shared, "seq", 2)
    hidden = call(
        functools.partial(finish_kernel, hops),
        [shape((total // 2, head), bf16)] * 2 if split else [shape((total, head), bf16)],
        2600000000,
        flags,
        queries,
        local,
        takes,
        norm_gain.reshape(1, head),
        other,
        *pairs,
    )
    out = shape((mine, width), bf16)
    if not split:
        mixed = lax.all_to_all(hidden[0].reshape(tp, -1, head), "tp", 0, 0, tiled=True)
        mixed = mixed.transpose(1, 0, 2).reshape(-1, tp * head)
        weight = lax.all_gather(out_weight, "tp", axis=0, tiled=True)
        tile = width // 4
        return pl.pallas_call(
            out_kernel,
            out_shape=out,
            grid=(width // tile,),
            in_specs=[
                pl.BlockSpec(mixed.shape, lambda i: (0, 0)),
                pl.BlockSpec((weight.shape[0], tile), lambda i: (0, i)),
            ],
            out_specs=pl.BlockSpec((mine, tile), lambda i: (0, i)),
        )(mixed, weight)
    near, far = hidden
    far = swap(far, "tp", 2)
    shared, shared_x, shared_z, rest = lax.optimization_barrier((shared, shared_x, shared_z, rest))
    sums, places = [], ((0, 3), (1, 2))
    for each, pieces in zip(places, ((shared, rest), (shared_x, shared_z))):
        columns = sum(w.shape[1] for w in pieces)
        own, beside = call(
            functools.partial(chip_kernel, each, piece),
            [shape((mine, columns), f32), shape((mine, columns), bf16)],
            8 * mine * head * columns,
            near,
            far,
            out_weight,
            *pieces,
        )
        sums += [own, swap(beside, "tp", 1)]
    return call(functools.partial(sum_kernel, places, piece), out, mine * width, *sums)


def solution(mesh):
    in_specs = (P(("seq", "tp"), None), P(None, "tp"), P("tp", None), P("tp"), P())
    out_specs = P(("seq", "tp"), None)
    return jax.shard_map(body, mesh=mesh, in_specs=in_specs, out_specs=out_specs, check_vma=False)
```

```python
import functools

import jax
import jax.numpy as jnp
from jax import lax
from jax.experimental import pallas as pl
from jax.experimental.pallas import tpu as pltpu
from jax.sharding import PartitionSpec as P

EPSILON = 1e-06
MOST = 1536

VMEM = pl.BlockSpec(memory_space=pltpu.VMEM)
SMEM = pl.BlockSpec(memory_space=pltpu.SMEM)


def doc_of(lengths_ref, position):
    end = jnp.int32(0)
    found = jnp.zeros_like(position)
    for d in range(lengths_ref.shape[0]):
        end = end + lengths_ref[d]
        found = found + (position >= end).astype(jnp.int32)
    return found


def mask_kernel(hops, source, lengths_ref, *refs):
    keep_refs, takes_ref, allowed_ref, flags_ref = refs[:-3], refs[-3], refs[-2], refs[-1]
    groups, (rows, lanes) = len(keep_refs), keep_refs[0].shape
    total = groups * rows
    index, me = lax.axis_index("seq"), lax.axis_index("tp")
    odd = lax.rem(index, 2) == 1
    first_doc = doc_of(lengths_ref, index * total)
    last_doc = doc_of(lengths_ref, (index + 1) * total - 1)

    def positions(shape, axis):
        row = lax.broadcasted_iota(jnp.int32, shape, axis)
        found = row + index * total
        if groups > 1:
            group = lax.div(row, rows)
            for j in range(groups):
                shift = (jnp.bitwise_xor(me, j) - j) * rows
                found = found + jnp.where(group == j, shift, 0)
        return found

    doc = doc_of(lengths_ref, positions((total, lanes), 0))
    takes_ref[...] = (doc == first_doc).astype(jnp.float32)
    keep = (doc == last_doc).astype(jnp.float32).astype(jnp.bfloat16)
    for j, ref in enumerate(keep_refs):
        ref[...] = keep[j * rows : (j + 1) * rows]
    to, of = positions((total, total), 0), positions((total, total), 1)
    allowed = (of <= to) & (doc_of(lengths_ref, of) == doc_of(lengths_ref, to))
    allowed_ref[...] = allowed.astype(jnp.float32).astype(jnp.bfloat16)

    def reaches(last, doc):
        return (last >= 0) & (doc_of(lengths_ref, last) == doc)

    pair = lax.div(index, 2)
    joined = reaches((2 * pair + 1) * total - 1, doc_of(lengths_ref, (2 * pair + 2) * total - 1))
    flags = [odd | joined, jnp.logical_not(odd) | joined, odd & reaches(index * total - 1, first_doc)]
    for k in range(1, hops + 1):
        sender = source(pair, k)
        flags.append((sender < pair) & reaches((sender + 1) * 2 * total - 1, first_doc))
    row = lax.broadcasted_iota(jnp.int32, flags_ref.shape, 0)
    found = jnp.zeros(flags_ref.shape, jnp.int32)
    for i, flag in enumerate(flags):
        found = found + jnp.where(row == i, flag.astype(jnp.int32), 0)
    flags_ref[...] = found.astype(jnp.float32)


def project_kernel(groups, before, first, weight_ref, *refs):
    rows, keep = refs[:groups], refs[groups : 2 * groups]
    out_ref, state_ref = refs[2 * groups + before :]
    head = keep[0].shape[1]
    found = jnp.dot(
        jnp.concatenate([r[...] for r in rows], axis=0),
        weight_ref[:, first:],
        preferred_element_type=jnp.float32,
    ).astype(jnp.bfloat16)
    out_ref[...] = found
    kept = jnp.concatenate([r[...] for r in keep], axis=0)
    keys, values = found[:, -2 * head : -head] * kept, found[:, -head:]
    state = lax.dot_general(
        keys, values, (((0,), (0,)), ((), ())), preferred_element_type=jnp.float32
    )
    if before:
        state = state + refs[2 * groups][...]
    state_ref[...] = state.astype(state_ref.dtype)


def local_kernel(groups, weight_ref, late_kv_ref, allowed_ref, *refs):
    rows, parts, query_ref, out_ref = refs[:groups], refs[groups:-2], refs[-2], refs[-1]
    head = weight_ref.shape[1] // 3
    late = jnp.dot(
        jnp.concatenate([r[...] for r in rows], axis=0),
        weight_ref[:, :head],
        preferred_element_type=jnp.float32,
    ).astype(jnp.bfloat16)
    queries = jnp.concatenate([r[:, :head] for r in parts] + [late], axis=0)
    query_ref[...] = queries
    keys = jnp.concatenate([r[:, head : 2 * head] for r in parts] + [late_kv_ref[:, :head]], axis=0)
    values = jnp.concatenate([r[:, 2 * head :] for r in parts] + [late_kv_ref[:, head:]], axis=0)
    scores = lax.dot_general(
        queries, keys, (((1,), (1,)), ((), ())), preferred_element_type=jnp.float32
    )
    scores = scores.astype(jnp.bfloat16) * allowed_ref[...]
    out_ref[...] = jnp.dot(scores, values, preferred_element_type=jnp.float32)


def pair_kernel(flags_ref, own_ref, other_ref, out_ref):
    out_ref[...] = (
        own_ref[...].astype(jnp.float32) * flags_ref[0:1, :]
        + other_ref[...].astype(jnp.float32) * flags_ref[1:2, :]
    ).astype(out_ref.dtype)


def finish_kernel(hops, flags_ref, query_ref, local_ref, takes_ref, gain_ref, *refs):
    state_refs, outs = refs[: hops + 1], refs[hops + 1 :]
    state = jnp.zeros(state_refs[0].shape, jnp.float32)
    for k, ref in enumerate(state_refs):
        state = state + ref[...].astype(jnp.float32) * flags_ref[2 + k : 3 + k, :]
    high = state.astype(jnp.bfloat16)
    low = (state - high.astype(jnp.float32)).astype(jnp.bfloat16)
    queries = query_ref[...]
    incoming = jnp.dot(queries, high, preferred_element_type=jnp.float32) + jnp.dot(
        queries, low, preferred_element_type=jnp.float32
    )
    attended = local_ref[...] + incoming * takes_ref[...]
    inverse_rms = lax.rsqrt(jnp.mean(attended * attended, axis=1, keepdims=True) + EPSILON)
    hidden = (attended * inverse_rms * gain_ref[...]).astype(jnp.bfloat16)
    each = hidden.shape[0] // len(outs)
    for j, out_ref in enumerate(outs):
        out_ref[...] = hidden[j * each : (j + 1) * each]


def piece_at(bits, width):
    place = jnp.bitwise_xor(lax.rem(lax.axis_index("seq"), 4), bits)
    return pl.ds(pl.multiple_of(place * width, 128), width)


def cut_kernel(weight_ref, shared_ref, rest_ref):
    piece = shared_ref.shape[1]
    shared_ref[...] = weight_ref[:, piece_at(0, piece)]
    rest_ref[:, :piece] = weight_ref[:, piece_at(3, piece)]
    rest_ref[:, piece:] = weight_ref[:, 4 * piece :]


def chip_kernel(places, piece, near_ref, far_ref, near_weight_ref, *refs):
    weights, (own_ref, other_ref) = refs[:-2], refs[-2:]
    rows = own_ref.shape[0]
    hidden = jnp.concatenate([near_ref[...], far_ref[...]], axis=1)
    done = 0
    for place, weight_ref in zip(places, weights):
        width = weight_ref.shape[1]
        near = near_weight_ref[:, piece_at(place, piece)]
        if width > piece:
            near = jnp.concatenate([near, near_weight_ref[:, 4 * piece :]], axis=1)
        weight = jnp.concatenate([near, weight_ref[...]], axis=0)
        result = jnp.dot(hidden, weight, preferred_element_type=jnp.float32)
        own_ref[:, done : done + width] = result[:rows]
        other_ref[:, done : done + width] = result[rows:].astype(other_ref.dtype)
        done += width


def sum_kernel(places, piece, *refs):
    out_ref = refs[-1]
    for each, own_ref, other_ref in zip(places, refs[:-1:2], refs[1:-1:2]):
        for k, place in enumerate(each):
            here = slice(k * piece, (k + 1) * piece)
            out_ref[:, piece_at(place, piece)] = (
                own_ref[:, here] + other_ref[:, here].astype(jnp.float32)
            ).astype(out_ref.dtype)
        if own_ref.shape[1] > len(each) * piece:
            out_ref[:, 4 * piece :] = (
                own_ref[:, len(each) * piece :]
                + other_ref[:, len(each) * piece :].astype(jnp.float32)
            ).astype(out_ref.dtype)


def out_kernel(hidden_ref, weight_ref, out_ref):
    out_ref[...] = jnp.dot(
        hidden_ref[...], weight_ref[...], preferred_element_type=jnp.float32
    ).astype(out_ref.dtype)


def call(kernel, out_shape, flops, *args, scalars=False):
    several = isinstance(out_shape, (list, tuple))
    return pl.pallas_call(
        kernel,
        out_shape=out_shape,
        in_specs=[SMEM if scalars and i == 0 else VMEM for i in range(len(args))],
        out_specs=[VMEM] * len(out_shape) if several else VMEM,
        cost_estimate=pl.CostEstimate(
            flops=flops,
            bytes_accessed=sum(a.size * a.dtype.itemsize for a in args) if flops else 0,
            transcendentals=0,
        ),
        compiler_params=pltpu.CompilerParams(vmem_limit_bytes=4 << 20),
    )(*args)


def swap(x, axis, bits):
    return lax.ppermute(x, axis, [(i, i ^ bits) for i in range(lax.axis_size(axis))])


def after(x, *others):
    return lax.optimization_barrier((x, *others))[0]


def body(tokens, qkv_weight, out_weight, norm_gain, doc_lengths):
    tp, seq = lax.axis_size("tp"), lax.axis_size("seq")
    head = qkv_weight.shape[1] // 3
    mine, width = tokens.shape[0], out_weight.shape[1]
    total = mine * tp
    bf16, f32 = jnp.bfloat16, jnp.float32
    shape = jax.ShapeDtypeStruct
    square = shape((head, head), bf16)
    split = tp == 4 and seq % 4 == 0
    groups = 4 if split else 1
    rows = total // groups
    piece = 7 * width // 32

    reach = -(-(MOST - 1) // total)
    hops = min(seq // 2 - 1, -(-reach // 2))
    everyone = seq == 8 and hops == 3
    *keep, takes, allowed, flags = call(
        functools.partial(mask_kernel, hops, jnp.bitwise_xor if everyone else jnp.subtract),
        [shape((rows, head), bf16)] * groups
        + [shape((total, head), f32), shape((total, total), bf16), shape((8, head), f32)],
        total * total,
        doc_lengths,
        scalars=True,
    )

    def project(x, group, *before, first=0, state_type=f32, cost=None):
        return call(
            functools.partial(project_kernel, len(x), len(before), first),
            [shape((len(x) * rows, 3 * head - first), bf16), shape((head, head), state_type)],
            6 * len(x) * x[0].size * head if cost is None else cost,
            qkv_weight,
            *x,
            *keep[group : group + len(x)],
            *before,
        )

    if split:
        across = swap(tokens, "tp", 2)
        own, state = project([tokens], 0)
        beside, state = project([swap(tokens, "tp", 1)], 1, state)
        shared, rest = call(
            cut_kernel,
            [shape((head, piece), bf16), shape((head, width - 3 * piece), bf16)],
            head * width,
            out_weight,
        )
        across, own, beside, state, shared, rest, takes, allowed, flags, *keep = (
            lax.optimization_barrier(
                (across, own, beside, state, shared, rest, takes, allowed, flags, *keep)
            )
        )
        late = [across, swap(across, "tp", 1)]
        shared = swap(shared, "tp", 2)
        parts, before = [own, beside], [state]
    else:
        late = [lax.all_gather(tokens, "tp", axis=0, tiled=True)]
        parts, before = [], []
    late_kv, tail = project(late, len(parts), *before, first=head, state_type=bf16)
    other = swap(tail, "seq", 1)
    queries, local = call(
        functools.partial(local_kernel, len(late)),
        [shape((total, head), bf16), shape((total, head), f32)],
        4 * total * total * head + 2 * len(late) * late[0].size * head,
        qkv_weight,
        late_kv,
        allowed,
        *late,
        *parts,
    )
    other = after(other, local)
    pair = call(pair_kernel, square, 1000000000, flags, tail, other)
    if everyone:
        pairs = [swap(pair, "seq", 2 * k) for k in range(1, hops + 1)]
    else:
        pairs = [
            lax.ppermute(pair, "seq", [(i, (i + 2 * k) % seq) for i in range(seq)])
            for k in range(1, hops + 1)
        ]
    if split:
        rest = swap(after(rest, local), "tp", 2)
        shared = after(shared, pair)
        shared_x, shared_z = swap(shared, "seq", 1), swap(shared, "seq", 2)
    hidden = call(
        functools.partial(finish_kernel, hops),
        [shape((total // 2, head), bf16)] * 2 if split else [shape((total, head), bf16)],
        2600000000,
        flags,
        queries,
        local,
        takes,
        norm_gain.reshape(1, head),
        other,
        *pairs,
    )
    out = shape((mine, width), bf16)
    if not split:
        mixed = lax.all_to_all(hidden[0].reshape(tp, -1, head), "tp", 0, 0, tiled=True)
        mixed = mixed.transpose(1, 0, 2).reshape(-1, tp * head)
        weight = lax.all_gather(out_weight, "tp", axis=0, tiled=True)
        tile = width // 4
        return pl.pallas_call(
            out_kernel,
            out_shape=out,
            grid=(width // tile,),
            in_specs=[
                pl.BlockSpec(mixed.shape, lambda i: (0, 0)),
                pl.BlockSpec((weight.shape[0], tile), lambda i: (0, i)),
            ],
            out_specs=pl.BlockSpec((mine, tile), lambda i: (0, i)),
        )(mixed, weight)
    near, far = hidden
    far = swap(far, "tp", 2)
    shared, shared_x, shared_z, rest = lax.optimization_barrier((shared, shared_x, shared_z, rest))
    sums, places = [], ((0, 3), (1, 2))
    for each, pieces in zip(places, ((shared, rest), (shared_x, shared_z))):
        columns = sum(w.shape[1] for w in pieces)
        own, beside = call(
            functools.partial(chip_kernel, each, piece),
            [shape((mine, columns), f32), shape((mine, columns), bf16)],
            8 * mine * head * columns,
            near,
            far,
            out_weight,
            *pieces,
        )
        sums += [own, swap(beside, "tp", 1)]
    return call(functools.partial(sum_kernel, places, piece), out, mine * width, *sums)


def solution(mesh):
    in_specs = (P(("seq", "tp"), None), P(None, "tp"), P("tp", None), P("tp"), P())
    out_specs = P(("seq", "tp"), None)
    return jax.shard_map(body, mesh=mesh, in_specs=in_specs, out_specs=out_specs, check_vma=False)
```

```python
import functools

import jax
import jax.numpy as jnp
from jax import lax
from jax.experimental import pallas as pl
from jax.experimental.pallas import tpu as pltpu
from jax.sharding import PartitionSpec as P

EPSILON = 1e-06
MOST = 1536
SHORT, LONG = 10**9, 3 * 10**9

VMEM = pl.BlockSpec(memory_space=pltpu.VMEM)
SMEM = pl.BlockSpec(memory_space=pltpu.SMEM)


def doc_of(lengths_ref, position):
    end = jnp.int32(0)
    found = jnp.zeros_like(position)
    for d in range(lengths_ref.shape[0]):
        end = end + lengths_ref[d]
        found = found + (position >= end).astype(jnp.int32)
    return found


def mask_kernel(hops, source, lengths_ref, *refs):
    keep_refs, takes_ref, allowed_ref, flags_ref = refs[:-3], refs[-3], refs[-2], refs[-1]
    groups, (rows, lanes) = len(keep_refs), keep_refs[0].shape
    total = groups * rows
    index, me = lax.axis_index("seq"), lax.axis_index("tp")
    odd = lax.rem(index, 2) == 1
    first_doc = doc_of(lengths_ref, index * total)
    last_doc = doc_of(lengths_ref, (index + 1) * total - 1)

    def positions(shape, axis):
        row = lax.broadcasted_iota(jnp.int32, shape, axis)
        found = row + index * total
        if groups > 1:
            group = lax.div(row, rows)
            for j in range(groups):
                shift = (jnp.bitwise_xor(me, j) - j) * rows
                found = found + jnp.where(group == j, shift, 0)
        return found

    doc = doc_of(lengths_ref, positions((total, lanes), 0))
    takes_ref[...] = (doc == first_doc).astype(jnp.float32)
    keep = (doc == last_doc).astype(jnp.float32).astype(jnp.bfloat16)
    for j, ref in enumerate(keep_refs):
        ref[...] = keep[j * rows : (j + 1) * rows]
    to, of = positions((total, total), 0), positions((total, total), 1)
    allowed = (of <= to) & (doc_of(lengths_ref, of) == doc_of(lengths_ref, to))
    allowed_ref[...] = allowed.astype(jnp.float32).astype(jnp.bfloat16)

    def reaches(last, doc):
        return (last >= 0) & (doc_of(lengths_ref, last) == doc)

    pair = lax.div(index, 2)
    joined = reaches((2 * pair + 1) * total - 1, doc_of(lengths_ref, (2 * pair + 2) * total - 1))
    flags = [odd | joined, jnp.logical_not(odd) | joined, odd & reaches(index * total - 1, first_doc)]
    for k in range(1, hops + 1):
        sender = source(pair, k)
        flags.append((sender < pair) & reaches((sender + 1) * 2 * total - 1, first_doc))
    row = lax.broadcasted_iota(jnp.int32, flags_ref.shape, 0)
    found = jnp.zeros(flags_ref.shape, jnp.int32)
    for i, flag in enumerate(flags):
        found = found + jnp.where(row == i, flag.astype(jnp.int32), 0)
    flags_ref[...] = found.astype(jnp.float32)


def project_kernel(groups, before, first, weight_ref, *refs):
    rows, keep = refs[:groups], refs[groups : 2 * groups]
    out_ref, state_ref = refs[2 * groups + before :]
    head = keep[0].shape[1]
    found = jnp.dot(
        jnp.concatenate([r[...] for r in rows], axis=0),
        weight_ref[:, first:],
        preferred_element_type=jnp.float32,
    ).astype(jnp.bfloat16)
    out_ref[...] = found
    kept = jnp.concatenate([r[...] for r in keep], axis=0)
    keys, values = found[:, -2 * head : -head] * kept, found[:, -head:]
    state = lax.dot_general(
        keys, values, (((0,), (0,)), ((), ())), preferred_element_type=jnp.float32
    )
    if before:
        state = state + refs[2 * groups][...]
    state_ref[...] = state.astype(state_ref.dtype)


def local_kernel(groups, weight_ref, late_kv_ref, allowed_ref, *refs):
    rows, parts, query_ref, out_ref = refs[:groups], refs[groups:-2], refs[-2], refs[-1]
    head = weight_ref.shape[1] // 3
    late = jnp.dot(
        jnp.concatenate([r[...] for r in rows], axis=0),
        weight_ref[:, :head],
        preferred_element_type=jnp.float32,
    ).astype(jnp.bfloat16)
    queries = jnp.concatenate([r[:, :head] for r in parts] + [late], axis=0)
    query_ref[...] = queries
    keys = jnp.concatenate([r[:, head : 2 * head] for r in parts] + [late_kv_ref[:, :head]], axis=0)
    values = jnp.concatenate([r[:, 2 * head :] for r in parts] + [late_kv_ref[:, head:]], axis=0)
    scores = lax.dot_general(
        queries, keys, (((1,), (1,)), ((), ())), preferred_element_type=jnp.float32
    )
    scores = scores.astype(jnp.bfloat16) * allowed_ref[...]
    out_ref[...] = jnp.dot(scores, values, preferred_element_type=jnp.float32)


def pair_kernel(flags_ref, own_ref, other_ref, out_ref):
    out_ref[...] = (
        own_ref[...].astype(jnp.float32) * flags_ref[0:1, :]
        + other_ref[...].astype(jnp.float32) * flags_ref[1:2, :]
    ).astype(out_ref.dtype)


def finish_kernel(order, flags_ref, query_ref, local_ref, takes_ref, gain_ref, *refs):
    state_refs, outs = refs[: len(order)], refs[len(order) :]
    state = jnp.zeros(state_refs[0].shape, jnp.float32)
    for k, ref in zip(order, state_refs):
        state = state + ref[...].astype(jnp.float32) * flags_ref[2 + k : 3 + k, :]
    high = state.astype(jnp.bfloat16)
    low = (state - high.astype(jnp.float32)).astype(jnp.bfloat16)
    queries = query_ref[...]
    incoming = jnp.dot(queries, high, preferred_element_type=jnp.float32) + jnp.dot(
        queries, low, preferred_element_type=jnp.float32
    )
    attended = local_ref[...] + incoming * takes_ref[...]
    inverse_rms = lax.rsqrt(jnp.mean(attended * attended, axis=1, keepdims=True) + EPSILON)
    hidden = (attended * inverse_rms * gain_ref[...]).astype(jnp.bfloat16)
    each = hidden.shape[0] // len(outs)
    for j, out_ref in enumerate(outs):
        out_ref[...] = hidden[j * each : (j + 1) * each]


def columns_of(place, piece):
    if place == 2:
        return slice(2 * piece, None)
    start = jnp.bitwise_xor(lax.rem(lax.axis_index("seq"), 2), place) * piece
    return pl.ds(pl.multiple_of(start, 128), piece)


def cut_kernel(weight_ref, shared_ref, rest_ref):
    piece = shared_ref.shape[1]
    shared_ref[...] = weight_ref[:, columns_of(0, piece)]
    rest_ref[...] = weight_ref[:, columns_of(2, piece)]


def chip_kernel(places, piece, near_ref, far_ref, near_weight_ref, *refs):
    weights, (own_ref, other_ref) = refs[:-2], refs[-2:]
    rows = own_ref.shape[0]
    hidden = jnp.concatenate([near_ref[...], far_ref[...]], axis=1)
    done = 0
    for place, weight_ref in zip(places, weights):
        width = weight_ref.shape[1]
        weight = jnp.concatenate(
            [near_weight_ref[:, columns_of(place, piece)], weight_ref[...]], axis=0
        )
        result = jnp.dot(hidden, weight, preferred_element_type=jnp.float32)
        own_ref[:, done : done + width] = result[:rows]
        other_ref[:, done : done + width] = result[rows:].astype(other_ref.dtype)
        done += width


def sum_kernel(places, piece, *refs):
    out_ref = refs[-1]
    for each, own_ref, other_ref in zip(places, refs[:-1:2], refs[1:-1:2]):
        done = 0
        for place in each:
            width = out_ref.shape[1] - 2 * piece if place == 2 else piece
            here = slice(done, done + width)
            out_ref[:, columns_of(place, piece)] = (
                own_ref[:, here] + other_ref[:, here].astype(jnp.float32)
            ).astype(out_ref.dtype)
            done += width


def out_kernel(hidden_ref, weight_ref, out_ref):
    out_ref[...] = jnp.dot(
        hidden_ref[...], weight_ref[...], preferred_element_type=jnp.float32
    ).astype(out_ref.dtype)


def call(kernel, out_shape, flops, *args, scalars=False):
    several = isinstance(out_shape, (list, tuple))
    return pl.pallas_call(
        kernel,
        out_shape=out_shape,
        in_specs=[SMEM if scalars and i == 0 else VMEM for i in range(len(args))],
        out_specs=[VMEM] * len(out_shape) if several else VMEM,
        cost_estimate=pl.CostEstimate(
            flops=flops,
            bytes_accessed=sum(a.size * a.dtype.itemsize for a in args) if flops else 0,
            transcendentals=0,
        ),
        compiler_params=pltpu.CompilerParams(vmem_limit_bytes=4 << 20),
    )(*args)


def swap(x, axis, bits):
    return lax.ppermute(x, axis, [(i, i ^ bits) for i in range(lax.axis_size(axis))])


def after(x, *others):
    return lax.optimization_barrier((x, *others))[0]


def body(tokens, qkv_weight, out_weight, norm_gain, doc_lengths):
    tp, seq = lax.axis_size("tp"), lax.axis_size("seq")
    head = qkv_weight.shape[1] // 3
    mine, width = tokens.shape[0], out_weight.shape[1]
    total = mine * tp
    bf16, f32 = jnp.bfloat16, jnp.float32
    shape = jax.ShapeDtypeStruct
    square = shape((head, head), bf16)
    split = tp == 4 and seq % 2 == 0
    groups = 4 if split else 1
    rows = total // groups
    piece = 5 * width // 16

    reach = -(-(MOST - 1) // total)
    hops = min(seq // 2 - 1, -(-reach // 2))
    everyone = seq == 8 and hops == 3
    *keep, takes, allowed, flags = call(
        functools.partial(mask_kernel, hops, jnp.bitwise_xor if everyone else jnp.subtract),
        [shape((rows, head), bf16)] * groups
        + [shape((total, head), f32), shape((total, total), bf16), shape((8, head), f32)],
        total * total,
        doc_lengths,
        scalars=True,
    )

    def project(x, group, *before, first=0, state_type=f32, cost=None):
        return call(
            functools.partial(project_kernel, len(x), len(before), first),
            [shape((len(x) * rows, 3 * head - first), bf16), shape((head, head), state_type)],
            6 * len(x) * x[0].size * head if cost is None else cost,
            qkv_weight,
            *x,
            *keep[group : group + len(x)],
            *before,
        )

    if split:
        across = swap(tokens, "tp", 2)
        own, state = project([tokens], 0)
        beside, state = project([swap(tokens, "tp", 1)], 1, state)
        shared, rest = call(
            cut_kernel,
            [shape((head, piece), bf16), shape((head, width - 2 * piece), bf16)],
            head * width,
            out_weight,
        )
        across, own, beside, state, shared, rest, takes, allowed, flags, *keep = (
            lax.optimization_barrier(
                (across, own, beside, state, shared, rest, takes, allowed, flags, *keep)
            )
        )
        late = [across, swap(across, "tp", 1)]
        shared = swap(shared, "tp", 2)
        parts, before = [own, beside], [state]
    else:
        late = [lax.all_gather(tokens, "tp", axis=0, tiled=True)]
        parts, before = [], []
    late_kv, tail = project(late, len(parts), *before, first=head, state_type=bf16)
    other = swap(tail, "seq", 1)
    queries, local = call(
        functools.partial(local_kernel, len(late)),
        [shape((total, head), bf16), shape((total, head), f32)],
        4 * total * total * head + 2 * len(late) * late[0].size * head,
        qkv_weight,
        late_kv,
        allowed,
        *late,
        *parts,
    )
    other = after(other, local)
    pair = call(pair_kernel, square, SHORT, flags, tail, other)
    if everyone:
        pairs = [swap(pair, "seq", 2 * k) for k in range(1, hops + 1)]
    else:
        pairs = [
            lax.ppermute(pair, "seq", [(i, (i + 2 * k) % seq) for i in range(seq)])
            for k in range(1, hops + 1)
        ]
    if split:
        rest = swap(after(rest, local), "tp", 2)
        shared_other = swap(after(shared, pair), "seq", 1)
    order = (0, 1, 3, 2) if everyone else tuple(range(hops + 1))
    hidden = call(
        functools.partial(finish_kernel, order),
        [shape((total // 2, head), bf16)] * 2 if split else [shape((total, head), bf16)],
        LONG,
        flags,
        queries,
        local,
        takes,
        norm_gain.reshape(1, head),
        *[([other] + pairs)[k] for k in order],
    )
    out = shape((mine, width), bf16)
    if not split:
        mixed = lax.all_to_all(hidden[0].reshape(tp, -1, head), "tp", 0, 0, tiled=True)
        mixed = mixed.transpose(1, 0, 2).reshape(-1, tp * head)
        weight = lax.all_gather(out_weight, "tp", axis=0, tiled=True)
        tile = width // 4
        return pl.pallas_call(
            out_kernel,
            out_shape=out,
            grid=(width // tile,),
            in_specs=[
                pl.BlockSpec(mixed.shape, lambda i: (0, 0)),
                pl.BlockSpec((weight.shape[0], tile), lambda i: (0, i)),
            ],
            out_specs=pl.BlockSpec((mine, tile), lambda i: (0, i)),
        )(mixed, weight)
    near, far = hidden
    far = swap(far, "tp", 2)
    sums, places = [], ((0, 2), (1,))
    for each, pieces in zip(places, ((shared, rest), (shared_other,))):
        columns = sum(w.shape[1] for w in pieces)
        own, beside = call(
            functools.partial(chip_kernel, each, piece),
            [shape((mine, columns), f32), shape((mine, columns), bf16)],
            8 * mine * head * columns,
            near,
            far,
            out_weight,
            *pieces,
        )
        sums += [own, swap(beside, "tp", 1)]
    return call(functools.partial(sum_kernel, places, piece), out, mine * width, *sums)


def solution(mesh):
    in_specs = (P(("seq", "tp"), None), P(None, "tp"), P("tp", None), P("tp"), P())
    out_specs = P(("seq", "tp"), None)
    return jax.shard_map(body, mesh=mesh, in_specs=in_specs, out_specs=out_specs, check_vma=False)
```

```python
import functools

import jax
import jax.numpy as jnp
from jax import lax
from jax.experimental import pallas as pl
from jax.experimental.pallas import tpu as pltpu
from jax.sharding import PartitionSpec as P

EPSILON = 1e-06
MOST = 1536
SHORT, LONG = 10**9, 3 * 10**9

VMEM = pl.BlockSpec(memory_space=pltpu.VMEM)
SMEM = pl.BlockSpec(memory_space=pltpu.SMEM)


def doc_of(lengths_ref, position):
    end = jnp.int32(0)
    found = jnp.zeros_like(position)
    for d in range(lengths_ref.shape[0]):
        end = end + lengths_ref[d]
        found = found + (position >= end).astype(jnp.int32)
    return found


def mask_kernel(hops, source, lengths_ref, *refs):
    keep_refs, takes_ref, allowed_ref, flags_ref = refs[:-3], refs[-3], refs[-2], refs[-1]
    groups, (rows, lanes) = len(keep_refs), keep_refs[0].shape
    total = groups * rows
    index, me = lax.axis_index("seq"), lax.axis_index("tp")
    odd = lax.rem(index, 2) == 1
    first_doc = doc_of(lengths_ref, index * total)
    last_doc = doc_of(lengths_ref, (index + 1) * total - 1)

    def positions(shape, axis):
        row = lax.broadcasted_iota(jnp.int32, shape, axis)
        found = row + index * total
        if groups > 1:
            group = lax.div(row, rows)
            for j in range(groups):
                shift = (jnp.bitwise_xor(me, j) - j) * rows
                found = found + jnp.where(group == j, shift, 0)
        return found

    doc = doc_of(lengths_ref, positions((total, lanes), 0))
    takes_ref[...] = (doc == first_doc).astype(jnp.float32)
    keep = (doc == last_doc).astype(jnp.float32).astype(jnp.bfloat16)
    for j, ref in enumerate(keep_refs):
        ref[...] = keep[j * rows : (j + 1) * rows]
    to, of = positions((total, total), 0), positions((total, total), 1)
    allowed = (of <= to) & (doc_of(lengths_ref, of) == doc_of(lengths_ref, to))
    allowed_ref[...] = allowed.astype(jnp.float32).astype(jnp.bfloat16)

    def reaches(last, doc):
        return (last >= 0) & (doc_of(lengths_ref, last) == doc)

    pair = lax.div(index, 2)
    joined = reaches((2 * pair + 1) * total - 1, doc_of(lengths_ref, (2 * pair + 2) * total - 1))
    flags = [odd | joined, jnp.logical_not(odd) | joined, odd & reaches(index * total - 1, first_doc)]
    for k in range(1, hops + 1):
        sender = source(pair, k)
        flags.append((sender < pair) & reaches((sender + 1) * 2 * total - 1, first_doc))
    row = lax.broadcasted_iota(jnp.int32, flags_ref.shape, 0)
    found = jnp.zeros(flags_ref.shape, jnp.int32)
    for i, flag in enumerate(flags):
        found = found + jnp.where(row == i, flag.astype(jnp.int32), 0)
    flags_ref[...] = found.astype(jnp.float32)


def project_kernel(groups, before, first, weight_ref, *refs):
    rows, keep = refs[:groups], refs[groups : 2 * groups]
    out_ref, state_ref = refs[2 * groups + before :]
    head = keep[0].shape[1]
    found = jnp.dot(
        jnp.concatenate([r[...] for r in rows], axis=0),
        weight_ref[:, first:],
        preferred_element_type=jnp.float32,
    ).astype(jnp.bfloat16)
    out_ref[...] = found
    kept = jnp.concatenate([r[...] for r in keep], axis=0)
    keys, values = found[:, -2 * head : -head] * kept, found[:, -head:]
    state = lax.dot_general(
        keys, values, (((0,), (0,)), ((), ())), preferred_element_type=jnp.float32
    )
    if before:
        state = state + refs[2 * groups][...]
    state_ref[...] = state.astype(state_ref.dtype)


def local_kernel(groups, weight_ref, late_kv_ref, allowed_ref, *refs):
    rows, parts, query_ref, out_ref = refs[:groups], refs[groups:-2], refs[-2], refs[-1]
    head = weight_ref.shape[1] // 3
    late = jnp.dot(
        jnp.concatenate([r[...] for r in rows], axis=0),
        weight_ref[:, :head],
        preferred_element_type=jnp.float32,
    ).astype(jnp.bfloat16)
    queries = jnp.concatenate([r[:, :head] for r in parts] + [late], axis=0)
    query_ref[...] = queries
    keys = jnp.concatenate([r[:, head : 2 * head] for r in parts] + [late_kv_ref[:, :head]], axis=0)
    values = jnp.concatenate([r[:, 2 * head :] for r in parts] + [late_kv_ref[:, head:]], axis=0)
    scores = lax.dot_general(
        queries, keys, (((1,), (1,)), ((), ())), preferred_element_type=jnp.float32
    )
    scores = scores.astype(jnp.bfloat16) * allowed_ref[...]
    out_ref[...] = jnp.dot(scores, values, preferred_element_type=jnp.float32)


def pair_kernel(flags_ref, own_ref, other_ref, out_ref):
    out_ref[...] = (
        own_ref[...].astype(jnp.float32) * flags_ref[0:1, :]
        + other_ref[...].astype(jnp.float32) * flags_ref[1:2, :]
    ).astype(out_ref.dtype)


def finish_kernel(order, flags_ref, query_ref, local_ref, takes_ref, gain_ref, *refs):
    state_refs, outs = refs[: len(order)], refs[len(order) :]
    state = jnp.zeros(state_refs[0].shape, jnp.float32)
    for k, ref in zip(order, state_refs):
        state = state + ref[...].astype(jnp.float32) * flags_ref[2 + k : 3 + k, :]
    high = state.astype(jnp.bfloat16)
    low = (state - high.astype(jnp.float32)).astype(jnp.bfloat16)
    queries = query_ref[...]
    incoming = jnp.dot(queries, high, preferred_element_type=jnp.float32) + jnp.dot(
        queries, low, preferred_element_type=jnp.float32
    )
    attended = local_ref[...] + incoming * takes_ref[...]
    inverse_rms = lax.rsqrt(jnp.mean(attended * attended, axis=1, keepdims=True) + EPSILON)
    hidden = (attended * inverse_rms * gain_ref[...]).astype(jnp.bfloat16)
    each = hidden.shape[0] // len(outs)
    for j, out_ref in enumerate(outs):
        out_ref[...] = hidden[j * each : (j + 1) * each]


def columns_of(place, piece):
    if place == 2:
        return slice(2 * piece, None)
    start = jnp.bitwise_xor(lax.rem(lax.axis_index("seq"), 2), place) * piece
    return pl.ds(pl.multiple_of(start, 128), piece)


def cut_kernel(weight_ref, shared_ref, rest_ref):
    piece = shared_ref.shape[1]
    shared_ref[...] = weight_ref[:, columns_of(0, piece)]
    rest_ref[...] = weight_ref[:, columns_of(2, piece)]


def chip_kernel(places, piece, near_ref, far_ref, near_weight_ref, *refs):
    weights, (own_ref, other_ref) = refs[:-2], refs[-2:]
    rows = own_ref.shape[0]
    hidden = jnp.concatenate([near_ref[...], far_ref[...]], axis=1)
    done = 0
    for place, weight_ref in zip(places, weights):
        width = weight_ref.shape[1]
        weight = jnp.concatenate(
            [near_weight_ref[:, columns_of(place, piece)], weight_ref[...]], axis=0
        )
        result = jnp.dot(hidden, weight, preferred_element_type=jnp.float32)
        own_ref[:, done : done + width] = result[:rows]
        other_ref[:, done : done + width] = result[rows:].astype(other_ref.dtype)
        done += width


def sum_kernel(places, piece, *refs):
    out_ref = refs[-1]
    for each, own_ref, other_ref in zip(places, refs[:-1:2], refs[1:-1:2]):
        done = 0
        for place in each:
            width = out_ref.shape[1] - 2 * piece if place == 2 else piece
            here = slice(done, done + width)
            out_ref[:, columns_of(place, piece)] = (
                own_ref[:, here] + other_ref[:, here].astype(jnp.float32)
            ).astype(out_ref.dtype)
            done += width


def out_kernel(hidden_ref, weight_ref, out_ref):
    out_ref[...] = jnp.dot(
        hidden_ref[...], weight_ref[...], preferred_element_type=jnp.float32
    ).astype(out_ref.dtype)


def call(kernel, out_shape, flops, *args, scalars=False):
    several = isinstance(out_shape, (list, tuple))
    return pl.pallas_call(
        kernel,
        out_shape=out_shape,
        in_specs=[SMEM if scalars and i == 0 else VMEM for i in range(len(args))],
        out_specs=[VMEM] * len(out_shape) if several else VMEM,
        cost_estimate=pl.CostEstimate(
            flops=flops,
            bytes_accessed=sum(a.size * a.dtype.itemsize for a in args) if flops else 0,
            transcendentals=0,
        ),
        compiler_params=pltpu.CompilerParams(vmem_limit_bytes=4 << 20),
    )(*args)


def swap(x, axis, bits):
    return lax.ppermute(x, axis, [(i, i ^ bits) for i in range(lax.axis_size(axis))])


def after(x, *others):
    return lax.optimization_barrier((x, *others))[0]


def body(tokens, qkv_weight, out_weight, norm_gain, doc_lengths):
    tp, seq = lax.axis_size("tp"), lax.axis_size("seq")
    head = qkv_weight.shape[1] // 3
    mine, width = tokens.shape[0], out_weight.shape[1]
    total = mine * tp
    bf16, f32 = jnp.bfloat16, jnp.float32
    shape = jax.ShapeDtypeStruct
    square = shape((head, head), bf16)
    split = tp == 4 and seq % 2 == 0
    groups = 4 if split else 1
    rows = total // groups
    piece = 5 * width // 16

    reach = -(-(MOST - 1) // total)
    hops = min(seq // 2 - 1, -(-reach // 2))
    everyone = seq == 8 and hops == 3
    *keep, takes, allowed, flags = call(
        functools.partial(mask_kernel, hops, jnp.bitwise_xor if everyone else jnp.subtract),
        [shape((rows, head), bf16)] * groups
        + [shape((total, head), f32), shape((total, total), bf16), shape((8, head), f32)],
        total * total,
        doc_lengths,
        scalars=True,
    )

    def project(x, group, *before, first=0, state_type=f32, cost=None):
        return call(
            functools.partial(project_kernel, len(x), len(before), first),
            [shape((len(x) * rows, 3 * head - first), bf16), shape((head, head), state_type)],
            6 * len(x) * x[0].size * head if cost is None else cost,
            qkv_weight,
            *x,
            *keep[group : group + len(x)],
            *before,
        )

    if split:
        across = swap(tokens, "tp", 2)
        own, state = project([tokens], 0)
        beside = swap(tokens, "tp", 1)
        shared, rest = call(
            cut_kernel,
            [shape((head, piece), bf16), shape((head, width - 2 * piece), bf16)],
            head * width,
            out_weight,
        )
        across, own, state, shared, rest, takes, allowed, flags, *keep = lax.optimization_barrier(
            (across, own, state, shared, rest, takes, allowed, flags, *keep)
        )
        late = [beside, across, swap(across, "tp", 1)]
        shared = swap(shared, "tp", 2)
        parts, before = [own], [state]
    else:
        late = [lax.all_gather(tokens, "tp", axis=0, tiled=True)]
        parts, before = [], []
    late_kv, tail = project(late, len(parts), *before, first=head, state_type=bf16)
    other = swap(tail, "seq", 1)
    queries, local = call(
        functools.partial(local_kernel, len(late)),
        [shape((total, head), bf16), shape((total, head), f32)],
        4 * total * total * head + 2 * len(late) * late[0].size * head,
        qkv_weight,
        late_kv,
        allowed,
        *late,
        *parts,
    )
    other = after(other, local)
    pair = call(pair_kernel, square, SHORT, flags, tail, other)
    if everyone:
        pairs = [swap(pair, "seq", 2 * k) for k in range(1, hops + 1)]
    else:
        pairs = [
            lax.ppermute(pair, "seq", [(i, (i + 2 * k) % seq) for i in range(seq)])
            for k in range(1, hops + 1)
        ]
    if split:
        rest = swap(after(rest, local), "tp", 2)
        shared_other = swap(after(shared, pair), "seq", 1)
    order = (0, 1, 3, 2) if everyone else tuple(range(hops + 1))
    hidden = call(
        functools.partial(finish_kernel, order),
        [shape((total // 2, head), bf16)] * 2 if split else [shape((total, head), bf16)],
        LONG,
        flags,
        queries,
        local,
        takes,
        norm_gain.reshape(1, head),
        *[([other] + pairs)[k] for k in order],
    )
    out = shape((mine, width), bf16)
    if not split:
        mixed = lax.all_to_all(hidden[0].reshape(tp, -1, head), "tp", 0, 0, tiled=True)
        mixed = mixed.transpose(1, 0, 2).reshape(-1, tp * head)
        weight = lax.all_gather(out_weight, "tp", axis=0, tiled=True)
        tile = width // 4
        return pl.pallas_call(
            out_kernel,
            out_shape=out,
            grid=(width // tile,),
            in_specs=[
                pl.BlockSpec(mixed.shape, lambda i: (0, 0)),
                pl.BlockSpec((weight.shape[0], tile), lambda i: (0, i)),
            ],
            out_specs=pl.BlockSpec((mine, tile), lambda i: (0, i)),
        )(mixed, weight)
    near, far = hidden
    far = swap(far, "tp", 2)
    sums, places = [], ((0, 2), (1,))
    for each, pieces in zip(places, ((shared, rest), (shared_other,))):
        columns = sum(w.shape[1] for w in pieces)
        own, beside = call(
            functools.partial(chip_kernel, each, piece),
            [shape((mine, columns), f32), shape((mine, columns), bf16)],
            8 * mine * head * columns,
            near,
            far,
            out_weight,
            *pieces,
        )
        sums += [own, swap(beside, "tp", 1)]
    return call(functools.partial(sum_kernel, places, piece), out, mine * width, *sums)


def solution(mesh):
    in_specs = (P(("seq", "tp"), None), P(None, "tp"), P("tp", None), P("tp"), P())
    out_specs = P(("seq", "tp"), None)
    return jax.shard_map(body, mesh=mesh, in_specs=in_specs, out_specs=out_specs, check_vma=False)
```

```python
import functools

import jax
import jax.numpy as jnp
from jax import lax
from jax.experimental import pallas as pl
from jax.experimental.pallas import tpu as pltpu
from jax.sharding import PartitionSpec as P

EPSILON = 1e-06
MOST = 1536
SHORT, LONG = 10**9, 3 * 10**9

VMEM = pl.BlockSpec(memory_space=pltpu.VMEM)
SMEM = pl.BlockSpec(memory_space=pltpu.SMEM)


def doc_of(lengths_ref, position):
    end = jnp.int32(0)
    found = jnp.zeros_like(position)
    for d in range(lengths_ref.shape[0]):
        end = end + lengths_ref[d]
        found = found + (position >= end).astype(jnp.int32)
    return found


def mask_kernel(hops, source, lengths_ref, *refs):
    keep_refs, takes_ref, allowed_ref, flags_ref = refs[:-3], refs[-3], refs[-2], refs[-1]
    groups, (rows, lanes) = len(keep_refs), keep_refs[0].shape
    total = groups * rows
    index, me = lax.axis_index("seq"), lax.axis_index("tp")
    odd = lax.rem(index, 2) == 1
    first_doc = doc_of(lengths_ref, index * total)
    last_doc = doc_of(lengths_ref, (index + 1) * total - 1)

    def positions(shape, axis):
        row = lax.broadcasted_iota(jnp.int32, shape, axis)
        found = row + index * total
        if groups > 1:
            group = lax.div(row, rows)
            for j in range(groups):
                shift = (jnp.bitwise_xor(me, j) - j) * rows
                found = found + jnp.where(group == j, shift, 0)
        return found

    doc = doc_of(lengths_ref, positions((total, lanes), 0))
    takes_ref[...] = (doc == first_doc).astype(jnp.float32)
    keep = (doc == last_doc).astype(jnp.float32).astype(jnp.bfloat16)
    for j, ref in enumerate(keep_refs):
        ref[...] = keep[j * rows : (j + 1) * rows]
    to, of = positions((total, total), 0), positions((total, total), 1)
    allowed = (of <= to) & (doc_of(lengths_ref, of) == doc_of(lengths_ref, to))
    allowed_ref[...] = allowed.astype(jnp.float32).astype(jnp.bfloat16)

    def reaches(last, doc):
        return (last >= 0) & (doc_of(lengths_ref, last) == doc)

    pair = lax.div(index, 2)
    joined = reaches((2 * pair + 1) * total - 1, doc_of(lengths_ref, (2 * pair + 2) * total - 1))
    flags = [odd | joined, jnp.logical_not(odd) | joined, odd & reaches(index * total - 1, first_doc)]
    for k in range(1, hops + 1):
        sender = source(pair, k)
        flags.append((sender < pair) & reaches((sender + 1) * 2 * total - 1, first_doc))
    row = lax.broadcasted_iota(jnp.int32, flags_ref.shape, 0)
    found = jnp.zeros(flags_ref.shape, jnp.int32)
    for i, flag in enumerate(flags):
        found = found + jnp.where(row == i, flag.astype(jnp.int32), 0)
    flags_ref[...] = found.astype(jnp.float32)


def project_kernel(parts, groups, before, first, weight_ref, *refs):
    rows, keep = refs[:parts], refs[parts : parts + groups]
    out_ref, state_ref = refs[parts + groups + before :]
    head = keep[0].shape[1]
    found = jnp.dot(
        jnp.concatenate([r[...] for r in rows], axis=0),
        weight_ref[:, first:],
        preferred_element_type=jnp.float32,
    ).astype(jnp.bfloat16)
    out_ref[...] = found
    kept = jnp.concatenate([r[...] for r in keep], axis=0)
    keys, values = found[:, -2 * head : -head] * kept, found[:, -head:]
    state = lax.dot_general(
        keys, values, (((0,), (0,)), ((), ())), preferred_element_type=jnp.float32
    )
    if before:
        state = state + refs[parts + groups][...]
    state_ref[...] = state.astype(state_ref.dtype)


def local_kernel(groups, weight_ref, late_kv_ref, allowed_ref, *refs):
    rows, parts, query_ref, out_ref = refs[:groups], refs[groups:-2], refs[-2], refs[-1]
    head = weight_ref.shape[1] // 3
    late = jnp.dot(
        jnp.concatenate([r[...] for r in rows], axis=0),
        weight_ref[:, :head],
        preferred_element_type=jnp.float32,
    ).astype(jnp.bfloat16)
    queries = jnp.concatenate([r[:, :head] for r in parts] + [late], axis=0)
    query_ref[...] = queries
    keys = jnp.concatenate([r[:, head : 2 * head] for r in parts] + [late_kv_ref[:, :head]], axis=0)
    values = jnp.concatenate([r[:, 2 * head :] for r in parts] + [late_kv_ref[:, head:]], axis=0)
    scores = lax.dot_general(
        queries, keys, (((1,), (1,)), ((), ())), preferred_element_type=jnp.float32
    )
    scores = scores.astype(jnp.bfloat16) * allowed_ref[...]
    out_ref[...] = jnp.dot(scores, values, preferred_element_type=jnp.float32)


def pair_kernel(flags_ref, own_ref, other_ref, out_ref):
    out_ref[...] = (
        own_ref[...].astype(jnp.float32) * flags_ref[0:1, :]
        + other_ref[...].astype(jnp.float32) * flags_ref[1:2, :]
    ).astype(out_ref.dtype)


def finish_kernel(order, flags_ref, query_ref, local_ref, takes_ref, gain_ref, *refs):
    state_refs, outs = refs[: len(order)], refs[len(order) :]
    state = jnp.zeros(state_refs[0].shape, jnp.float32)
    for k, ref in zip(order, state_refs):
        state = state + ref[...].astype(jnp.float32) * flags_ref[2 + k : 3 + k, :]
    high = state.astype(jnp.bfloat16)
    low = (state - high.astype(jnp.float32)).astype(jnp.bfloat16)
    queries = query_ref[...]
    incoming = jnp.dot(queries, high, preferred_element_type=jnp.float32) + jnp.dot(
        queries, low, preferred_element_type=jnp.float32
    )
    attended = local_ref[...] + incoming * takes_ref[...]
    inverse_rms = lax.rsqrt(jnp.mean(attended * attended, axis=1, keepdims=True) + EPSILON)
    hidden = (attended * inverse_rms * gain_ref[...]).astype(jnp.bfloat16)
    each = hidden.shape[0] // len(outs)
    for j, out_ref in enumerate(outs):
        out_ref[...] = hidden[j * each : (j + 1) * each]


def columns_of(place, piece):
    if place == 2:
        return slice(2 * piece, None)
    start = jnp.bitwise_xor(lax.rem(lax.axis_index("seq"), 2), place) * piece
    return pl.ds(pl.multiple_of(start, 128), piece)


def halve_kernel(rows_ref, first_ref, second_ref):
    half = first_ref.shape[0]
    first_ref[...] = rows_ref[:half]
    second_ref[...] = rows_ref[half:]


def cut_kernel(weight_ref, shared_ref, rest_ref):
    piece = shared_ref.shape[1]
    shared_ref[...] = weight_ref[:, columns_of(0, piece)]
    rest_ref[...] = weight_ref[:, columns_of(2, piece)]


def chip_kernel(places, piece, near_ref, far_ref, near_weight_ref, *refs):
    weights, (own_ref, other_ref) = refs[:-2], refs[-2:]
    rows = own_ref.shape[0]
    hidden = jnp.concatenate([near_ref[...], far_ref[...]], axis=1)
    done = 0
    for place, weight_ref in zip(places, weights):
        width = weight_ref.shape[1]
        weight = jnp.concatenate(
            [near_weight_ref[:, columns_of(place, piece)], weight_ref[...]], axis=0
        )
        result = jnp.dot(hidden, weight, preferred_element_type=jnp.float32)
        own_ref[:, done : done + width] = result[:rows]
        other_ref[:, done : done + width] = result[rows:].astype(other_ref.dtype)
        done += width


def sum_kernel(places, piece, *refs):
    out_ref = refs[-1]
    for each, own_ref, other_ref in zip(places, refs[:-1:2], refs[1:-1:2]):
        done = 0
        for place in each:
            width = out_ref.shape[1] - 2 * piece if place == 2 else piece
            here = slice(done, done + width)
            out_ref[:, columns_of(place, piece)] = (
                own_ref[:, here] + other_ref[:, here].astype(jnp.float32)
            ).astype(out_ref.dtype)
            done += width


def out_kernel(hidden_ref, weight_ref, out_ref):
    out_ref[...] = jnp.dot(
        hidden_ref[...], weight_ref[...], preferred_element_type=jnp.float32
    ).astype(out_ref.dtype)


def call(kernel, out_shape, flops, *args, scalars=False):
    several = isinstance(out_shape, (list, tuple))
    return pl.pallas_call(
        kernel,
        out_shape=out_shape,
        in_specs=[SMEM if scalars and i == 0 else VMEM for i in range(len(args))],
        out_specs=[VMEM] * len(out_shape) if several else VMEM,
        cost_estimate=pl.CostEstimate(
            flops=flops,
            bytes_accessed=sum(a.size * a.dtype.itemsize for a in args) if flops else 0,
            transcendentals=0,
        ),
        compiler_params=pltpu.CompilerParams(vmem_limit_bytes=4 << 20),
    )(*args)


def swap(x, axis, bits):
    return lax.ppermute(x, axis, [(i, i ^ bits) for i in range(lax.axis_size(axis))])


def after(x, *others):
    return lax.optimization_barrier((x, *others))[0]


def body(tokens, qkv_weight, out_weight, norm_gain, doc_lengths):
    tp, seq = lax.axis_size("tp"), lax.axis_size("seq")
    head = qkv_weight.shape[1] // 3
    mine, width = tokens.shape[0], out_weight.shape[1]
    total = mine * tp
    bf16, f32 = jnp.bfloat16, jnp.float32
    shape = jax.ShapeDtypeStruct
    square = shape((head, head), bf16)
    split = tp == 4 and seq % 2 == 0
    groups = 4 if split else 1
    rows = total // groups
    piece = 5 * width // 16

    reach = -(-(MOST - 1) // total)
    hops = min(seq // 2 - 1, -(-reach // 2))
    everyone = seq == 8 and hops == 3
    *keep, takes, allowed, flags = call(
        functools.partial(mask_kernel, hops, jnp.bitwise_xor if everyone else jnp.subtract),
        [shape((rows, head), bf16)] * groups
        + [shape((total, head), f32), shape((total, total), bf16), shape((8, head), f32)],
        total * total,
        doc_lengths,
        scalars=True,
    )

    def project(x, group, *before, first=0, state_type=f32):
        found = sum(part.shape[0] for part in x)
        kept = keep[group : group + found // rows]
        return call(
            functools.partial(project_kernel, len(x), len(kept), len(before), first),
            [shape((found, 3 * head - first), bf16), shape((head, head), state_type)],
            6 * found * tokens.shape[1] * head,
            qkv_weight,
            *x,
            *kept,
            *before,
        )

    if split:
        across = swap(tokens, "tp", 2)
        own, state = project([tokens], 0)
        halves = call(halve_kernel, [shape((mine // 2, tokens.shape[1]), bf16)] * 2, 0, tokens)
        beside, state = project([swap(half, "tp", 1) for half in halves], 1, state)
        shared, rest = call(
            cut_kernel,
            [shape((head, piece), bf16), shape((head, width - 2 * piece), bf16)],
            head * width,
            out_weight,
        )
        across, own, beside, state, shared, rest, takes, allowed, flags, *keep = (
            lax.optimization_barrier(
                (across, own, beside, state, shared, rest, takes, allowed, flags, *keep)
            )
        )
        late = [across, swap(across, "tp", 1)]
        shared = swap(shared, "tp", 2)
        parts, before = [own, beside], [state]
    else:
        late = [lax.all_gather(tokens, "tp", axis=0, tiled=True)]
        parts, before = [], []
    late_kv, tail = project(late, len(parts), *before, first=head, state_type=bf16)
    other = swap(tail, "seq", 1)
    queries, local = call(
        functools.partial(local_kernel, len(late)),
        [shape((total, head), bf16), shape((total, head), f32)],
        4 * total * total * head + 2 * len(late) * late[0].size * head,
        qkv_weight,
        late_kv,
        allowed,
        *late,
        *parts,
    )
    other = after(other, local)
    pair = call(pair_kernel, square, SHORT, flags, tail, other)
    if everyone:
        pairs = [swap(pair, "seq", 2 * k) for k in range(1, hops + 1)]
    else:
        pairs = [
            lax.ppermute(pair, "seq", [(i, (i + 2 * k) % seq) for i in range(seq)])
            for k in range(1, hops + 1)
        ]
    if split:
        rest = swap(after(rest, local), "tp", 2)
        shared_other = swap(after(shared, pair), "seq", 1)
    order = (0, 1, 3, 2) if everyone else tuple(range(hops + 1))
    hidden = call(
        functools.partial(finish_kernel, order),
        [shape((total // 2, head), bf16)] * 2 if split else [shape((total, head), bf16)],
        LONG,
        flags,
        queries,
        local,
        takes,
        norm_gain.reshape(1, head),
        *[([other] + pairs)[k] for k in order],
    )
    out = shape((mine, width), bf16)
    if not split:
        mixed = lax.all_to_all(hidden[0].reshape(tp, -1, head), "tp", 0, 0, tiled=True)
        mixed = mixed.transpose(1, 0, 2).reshape(-1, tp * head)
        weight = lax.all_gather(out_weight, "tp", axis=0, tiled=True)
        tile = width // 4
        return pl.pallas_call(
            out_kernel,
            out_shape=out,
            grid=(width // tile,),
            in_specs=[
                pl.BlockSpec(mixed.shape, lambda i: (0, 0)),
                pl.BlockSpec((weight.shape[0], tile), lambda i: (0, i)),
            ],
            out_specs=pl.BlockSpec((mine, tile), lambda i: (0, i)),
        )(mixed, weight)
    near, far = hidden
    far = swap(far, "tp", 2)
    sums, places = [], ((0, 2), (1,))
    for each, pieces in zip(places, ((shared, rest), (shared_other,))):
        columns = sum(w.shape[1] for w in pieces)
        own, beside = call(
            functools.partial(chip_kernel, each, piece),
            [shape((mine, columns), f32), shape((mine, columns), bf16)],
            8 * mine * head * columns,
            near,
            far,
            out_weight,
            *pieces,
        )
        sums += [own, swap(beside, "tp", 1)]
    return call(functools.partial(sum_kernel, places, piece), out, mine * width, *sums)


def solution(mesh):
    in_specs = (P(("seq", "tp"), None), P(None, "tp"), P("tp", None), P("tp"), P())
    out_specs = P(("seq", "tp"), None)
    return jax.shard_map(body, mesh=mesh, in_specs=in_specs, out_specs=out_specs, check_vma=False)
```

```python
import functools

import jax
import jax.numpy as jnp
from jax import lax
from jax.experimental import pallas as pl
from jax.experimental.pallas import tpu as pltpu
from jax.sharding import PartitionSpec as P

EPSILON = 1e-06
MOST = 1536
SHORT, LONG = 10**9, 3 * 10**9

VMEM = pl.BlockSpec(memory_space=pltpu.VMEM)
SMEM = pl.BlockSpec(memory_space=pltpu.SMEM)


def doc_of(lengths_ref, position):
    end = jnp.int32(0)
    found = jnp.zeros_like(position)
    for d in range(lengths_ref.shape[0]):
        end = end + lengths_ref[d]
        found = found + (position >= end).astype(jnp.int32)
    return found


def mask_kernel(hops, source, lengths_ref, *refs):
    keep_refs, takes_ref, allowed_ref, flags_ref = refs[:-3], refs[-3], refs[-2], refs[-1]
    groups, (rows, lanes) = len(keep_refs), keep_refs[0].shape
    total = groups * rows
    index, me = lax.axis_index("seq"), lax.axis_index("tp")
    odd = lax.rem(index, 2) == 1
    first_doc = doc_of(lengths_ref, index * total)
    last_doc = doc_of(lengths_ref, (index + 1) * total - 1)

    def positions(shape, axis):
        row = lax.broadcasted_iota(jnp.int32, shape, axis)
        found = row + index * total
        if groups > 1:
            group = lax.div(row, rows)
            for j in range(groups):
                shift = (jnp.bitwise_xor(me, j) - j) * rows
                found = found + jnp.where(group == j, shift, 0)
        return found

    doc = doc_of(lengths_ref, positions((total, lanes), 0))
    takes_ref[...] = (doc == first_doc).astype(jnp.float32)
    keep = (doc == last_doc).astype(jnp.float32).astype(jnp.bfloat16)
    for j, ref in enumerate(keep_refs):
        ref[...] = keep[j * rows : (j + 1) * rows]
    to, of = positions((total, total), 0), positions((total, total), 1)
    allowed = (of <= to) & (doc_of(lengths_ref, of) == doc_of(lengths_ref, to))
    allowed_ref[...] = allowed.astype(jnp.float32).astype(jnp.bfloat16)

    def reaches(last, doc):
        return (last >= 0) & (doc_of(lengths_ref, last) == doc)

    pair = lax.div(index, 2)
    joined = reaches((2 * pair + 1) * total - 1, doc_of(lengths_ref, (2 * pair + 2) * total - 1))
    flags = [odd | joined, jnp.logical_not(odd) | joined, odd & reaches(index * total - 1, first_doc)]
    for k in range(1, hops + 1):
        sender = source(pair, k)
        flags.append((sender < pair) & reaches((sender + 1) * 2 * total - 1, first_doc))
    row = lax.broadcasted_iota(jnp.int32, flags_ref.shape, 0)
    found = jnp.zeros(flags_ref.shape, jnp.int32)
    for i, flag in enumerate(flags):
        found = found + jnp.where(row == i, flag.astype(jnp.int32), 0)
    flags_ref[...] = found.astype(jnp.float32)


def project_kernel(parts, groups, before, first, weight_ref, *refs):
    rows, keep = refs[:parts], refs[parts : parts + groups]
    out_ref, state_ref = refs[parts + groups + before :]
    head = keep[0].shape[1]
    found = jnp.dot(
        jnp.concatenate([r[...] for r in rows], axis=0),
        weight_ref[:, first:],
        preferred_element_type=jnp.float32,
    ).astype(jnp.bfloat16)
    out_ref[...] = found
    kept = jnp.concatenate([r[...] for r in keep], axis=0)
    keys, values = found[:, -2 * head : -head] * kept, found[:, -head:]
    state = lax.dot_general(
        keys, values, (((0,), (0,)), ((), ())), preferred_element_type=jnp.float32
    )
    if before:
        state = state + refs[parts + groups][...]
    state_ref[...] = state.astype(state_ref.dtype)


def local_kernel(groups, weight_ref, late_kv_ref, allowed_ref, *refs):
    rows, parts, query_ref, out_ref = refs[:groups], refs[groups:-2], refs[-2], refs[-1]
    head = weight_ref.shape[1] // 3
    late = jnp.dot(
        jnp.concatenate([r[...] for r in rows], axis=0),
        weight_ref[:, :head],
        preferred_element_type=jnp.float32,
    ).astype(jnp.bfloat16)
    queries = jnp.concatenate([r[:, :head] for r in parts] + [late], axis=0)
    query_ref[...] = queries
    keys = jnp.concatenate([r[:, head : 2 * head] for r in parts] + [late_kv_ref[:, :head]], axis=0)
    values = jnp.concatenate([r[:, 2 * head :] for r in parts] + [late_kv_ref[:, head:]], axis=0)
    scores = lax.dot_general(
        queries, keys, (((1,), (1,)), ((), ())), preferred_element_type=jnp.float32
    )
    scores = scores.astype(jnp.bfloat16) * allowed_ref[...]
    out_ref[...] = jnp.dot(scores, values, preferred_element_type=jnp.float32)


def pair_kernel(flags_ref, own_ref, other_ref, out_ref):
    out_ref[...] = (
        own_ref[...].astype(jnp.float32) * flags_ref[0:1, :]
        + other_ref[...].astype(jnp.float32) * flags_ref[1:2, :]
    ).astype(out_ref.dtype)


def finish_kernel(order, flags_ref, query_ref, local_ref, takes_ref, gain_ref, *refs):
    state_refs, outs = refs[: len(order)], refs[len(order) :]
    state = jnp.zeros(state_refs[0].shape, jnp.float32)
    for k, ref in zip(order, state_refs):
        state = state + ref[...].astype(jnp.float32) * flags_ref[2 + k : 3 + k, :]
    high = state.astype(jnp.bfloat16)
    low = (state - high.astype(jnp.float32)).astype(jnp.bfloat16)
    queries = query_ref[...]
    incoming = jnp.dot(queries, high, preferred_element_type=jnp.float32) + jnp.dot(
        queries, low, preferred_element_type=jnp.float32
    )
    attended = local_ref[...] + incoming * takes_ref[...]
    inverse_rms = lax.rsqrt(jnp.mean(attended * attended, axis=1, keepdims=True) + EPSILON)
    hidden = (attended * inverse_rms * gain_ref[...]).astype(jnp.bfloat16)
    each = hidden.shape[0] // len(outs)
    for j, out_ref in enumerate(outs):
        out_ref[...] = hidden[j * each : (j + 1) * each]


def columns_of(place, piece):
    if place == 2:
        return slice(2 * piece, None)
    start = jnp.bitwise_xor(lax.rem(lax.axis_index("seq"), 2), place) * piece
    return pl.ds(pl.multiple_of(start, 128), piece)


def halve_kernel(rows_ref, first_ref, second_ref):
    half = first_ref.shape[0]
    first_ref[...] = rows_ref[:half]
    second_ref[...] = rows_ref[half:]


def cut_kernel(weight_ref, shared_ref, rest_ref):
    piece = shared_ref.shape[1]
    shared_ref[...] = weight_ref[:, columns_of(0, piece)]
    rest_ref[...] = weight_ref[:, columns_of(2, piece)]


def chip_kernel(places, piece, near_ref, far_ref, near_weight_ref, *refs):
    weights, (own_ref, other_ref) = refs[:-2], refs[-2:]
    rows = own_ref.shape[0]
    hidden = jnp.concatenate([near_ref[...], far_ref[...]], axis=1)
    done = 0
    for place, weight_ref in zip(places, weights):
        width = weight_ref.shape[1]
        weight = jnp.concatenate(
            [near_weight_ref[:, columns_of(place, piece)], weight_ref[...]], axis=0
        )
        result = jnp.dot(hidden, weight, preferred_element_type=jnp.float32)
        own_ref[:, done : done + width] = result[:rows]
        other_ref[:, done : done + width] = result[rows:].astype(other_ref.dtype)
        done += width


def sum_kernel(places, piece, *refs):
    parts, out_ref, held, sems = refs[:-3], refs[-3], refs[-2], refs[-1]
    copies, at = [], 0
    for each, own_ref, other_ref in zip(places, parts[::2], parts[1::2]):
        done = 0
        for place in each:
            width = held.shape[1] - 2 * piece if place == 2 else piece
            here, there = slice(done, done + width), slice(at, at + width)
            held[:, there] = (
                own_ref[:, here] + other_ref[:, here].astype(jnp.float32)
            ).astype(held.dtype)
            target = out_ref.at[:, columns_of(place, piece)]
            copies.append(pltpu.make_async_copy(held.at[:, there], target, sems.at[len(copies)]))
            copies[-1].start()
            done, at = done + width, at + width
    for copy in copies:
        copy.wait()


def out_kernel(hidden_ref, weight_ref, out_ref):
    out_ref[...] = jnp.dot(
        hidden_ref[...], weight_ref[...], preferred_element_type=jnp.float32
    ).astype(out_ref.dtype)


def call(kernel, out_shape, flops, *args, scalars=False):
    several = isinstance(out_shape, (list, tuple))
    return pl.pallas_call(
        kernel,
        out_shape=out_shape,
        in_specs=[SMEM if scalars and i == 0 else VMEM for i in range(len(args))],
        out_specs=[VMEM] * len(out_shape) if several else VMEM,
        cost_estimate=pl.CostEstimate(
            flops=flops,
            bytes_accessed=sum(a.size * a.dtype.itemsize for a in args) if flops else 0,
            transcendentals=0,
        ),
        compiler_params=pltpu.CompilerParams(vmem_limit_bytes=4 << 20),
    )(*args)


def swap(x, axis, bits):
    return lax.ppermute(x, axis, [(i, i ^ bits) for i in range(lax.axis_size(axis))])


def after(x, *others):
    return lax.optimization_barrier((x, *others))[0]


def body(tokens, qkv_weight, out_weight, norm_gain, doc_lengths):
    tp, seq = lax.axis_size("tp"), lax.axis_size("seq")
    head = qkv_weight.shape[1] // 3
    mine, width = tokens.shape[0], out_weight.shape[1]
    total = mine * tp
    bf16, f32 = jnp.bfloat16, jnp.float32
    shape = jax.ShapeDtypeStruct
    square = shape((head, head), bf16)
    split = tp == 4 and seq % 2 == 0
    groups = 4 if split else 1
    rows = total // groups
    piece = 5 * width // 16

    reach = -(-(MOST - 1) // total)
    hops = min(seq // 2 - 1, -(-reach // 2))
    everyone = seq == 8 and hops == 3
    *keep, takes, allowed, flags = call(
        functools.partial(mask_kernel, hops, jnp.bitwise_xor if everyone else jnp.subtract),
        [shape((rows, head), bf16)] * groups
        + [shape((total, head), f32), shape((total, total), bf16), shape((8, head), f32)],
        total * total,
        doc_lengths,
        scalars=True,
    )

    def project(x, group, *before, first=0, state_type=f32):
        found = sum(part.shape[0] for part in x)
        kept = keep[group : group + found // rows]
        return call(
            functools.partial(project_kernel, len(x), len(kept), len(before), first),
            [shape((found, 3 * head - first), bf16), shape((head, head), state_type)],
            6 * found * tokens.shape[1] * head,
            qkv_weight,
            *x,
            *kept,
            *before,
        )

    if split:
        across = swap(tokens, "tp", 2)
        own, state = project([tokens], 0)
        halves = call(halve_kernel, [shape((mine // 2, tokens.shape[1]), bf16)] * 2, 0, tokens)
        beside, state = project([swap(half, "tp", 1) for half in halves], 1, state)
        shared, rest = call(
            cut_kernel,
            [shape((head, piece), bf16), shape((head, width - 2 * piece), bf16)],
            head * width,
            out_weight,
        )
        across, own, beside, state, shared, rest, takes, allowed, flags, *keep = (
            lax.optimization_barrier(
                (across, own, beside, state, shared, rest, takes, allowed, flags, *keep)
            )
        )
        late = [across, swap(across, "tp", 1)]
        shared = swap(shared, "tp", 2)
        parts, before = [own, beside], [state]
    else:
        late = [lax.all_gather(tokens, "tp", axis=0, tiled=True)]
        parts, before = [], []
    late_kv, tail = project(late, len(parts), *before, first=head, state_type=bf16)
    other = swap(tail, "seq", 1)
    queries, local = call(
        functools.partial(local_kernel, len(late)),
        [shape((total, head), bf16), shape((total, head), f32)],
        4 * total * total * head + 2 * len(late) * late[0].size * head,
        qkv_weight,
        late_kv,
        allowed,
        *late,
        *parts,
    )
    other = after(other, local)
    pair = call(pair_kernel, square, SHORT, flags, tail, other)
    if everyone:
        pairs = [swap(pair, "seq", 2 * k) for k in range(1, hops + 1)]
    else:
        pairs = [
            lax.ppermute(pair, "seq", [(i, (i + 2 * k) % seq) for i in range(seq)])
            for k in range(1, hops + 1)
        ]
    if split:
        rest = swap(after(rest, local), "tp", 2)
        shared_other = swap(after(shared, pair), "seq", 1)
    order = (0, 1, 3, 2) if everyone else tuple(range(hops + 1))
    hidden = call(
        functools.partial(finish_kernel, order),
        [shape((total // 2, head), bf16)] * 2 if split else [shape((total, head), bf16)],
        LONG,
        flags,
        queries,
        local,
        takes,
        norm_gain.reshape(1, head),
        *[([other] + pairs)[k] for k in order],
    )
    out = shape((mine, width), bf16)
    if not split:
        mixed = lax.all_to_all(hidden[0].reshape(tp, -1, head), "tp", 0, 0, tiled=True)
        mixed = mixed.transpose(1, 0, 2).reshape(-1, tp * head)
        weight = lax.all_gather(out_weight, "tp", axis=0, tiled=True)
        tile = width // 4
        return pl.pallas_call(
            out_kernel,
            out_shape=out,
            grid=(width // tile,),
            in_specs=[
                pl.BlockSpec(mixed.shape, lambda i: (0, 0)),
                pl.BlockSpec((weight.shape[0], tile), lambda i: (0, i)),
            ],
            out_specs=pl.BlockSpec((mine, tile), lambda i: (0, i)),
        )(mixed, weight)
    near, far = hidden
    far = swap(far, "tp", 2)
    sums, places = [], ((0, 2), (1,))
    for each, pieces in zip(places, ((shared, rest), (shared_other,))):
        columns = sum(w.shape[1] for w in pieces)
        own, beside = call(
            functools.partial(chip_kernel, each, piece),
            [shape((mine, columns), f32), shape((mine, columns), bf16)],
            8 * mine * head * columns,
            near,
            far,
            out_weight,
            *pieces,
        )
        sums += [own, swap(beside, "tp", 1)]
    return pl.pallas_call(
        functools.partial(sum_kernel, places, piece),
        out_shape=out,
        in_specs=[VMEM] * len(sums),
        out_specs=pl.BlockSpec(memory_space=pltpu.HBM),
        scratch_shapes=[pltpu.VMEM((mine, width), bf16), pltpu.SemaphoreType.DMA((3,))],
        cost_estimate=pl.CostEstimate(
            flops=mine * width, bytes_accessed=7 * mine * width, transcendentals=0
        ),
        compiler_params=pltpu.CompilerParams(vmem_limit_bytes=4 << 20),
    )(*sums)


def solution(mesh):
    in_specs = (P(("seq", "tp"), None), P(None, "tp"), P("tp", None), P("tp"), P())
    out_specs = P(("seq", "tp"), None)
    return jax.shard_map(body, mesh=mesh, in_specs=in_specs, out_specs=out_specs, check_vma=False)
```

```python
import functools

import jax
import jax.numpy as jnp
from jax import lax
from jax.experimental import pallas as pl
from jax.experimental.pallas import tpu as pltpu
from jax.sharding import PartitionSpec as P

EPSILON = 1e-06
MOST = 1536
SHORT, LONG = 10**9, 3 * 10**9

VMEM = pl.BlockSpec(memory_space=pltpu.VMEM)
SMEM = pl.BlockSpec(memory_space=pltpu.SMEM)


def doc_of(lengths_ref, position):
    end = jnp.int32(0)
    found = jnp.zeros_like(position)
    for d in range(lengths_ref.shape[0]):
        end = end + lengths_ref[d]
        found = found + (position >= end).astype(jnp.int32)
    return found


def mask_kernel(hops, source, lengths_ref, *refs):
    keep_refs, takes_ref, allowed_ref, flags_ref = refs[:-3], refs[-3], refs[-2], refs[-1]
    groups, (rows, lanes) = len(keep_refs), keep_refs[0].shape
    total = groups * rows
    index, me = lax.axis_index("seq"), lax.axis_index("tp")
    odd = lax.rem(index, 2) == 1
    first_doc = doc_of(lengths_ref, index * total)
    last_doc = doc_of(lengths_ref, (index + 1) * total - 1)

    def positions(shape, axis):
        row = lax.broadcasted_iota(jnp.int32, shape, axis)
        found = row + index * total
        if groups > 1:
            group = lax.div(row, rows)
            for j in range(groups):
                shift = (jnp.bitwise_xor(me, j) - j) * rows
                found = found + jnp.where(group == j, shift, 0)
        return found

    doc = doc_of(lengths_ref, positions((total, lanes), 0))
    takes_ref[...] = (doc == first_doc).astype(jnp.float32)
    keep = (doc == last_doc).astype(jnp.float32).astype(jnp.bfloat16)
    for j, ref in enumerate(keep_refs):
        ref[...] = keep[j * rows : (j + 1) * rows]
    to, of = positions((total, total), 0), positions((total, total), 1)
    allowed = (of <= to) & (doc_of(lengths_ref, of) == doc_of(lengths_ref, to))
    allowed_ref[...] = allowed.astype(jnp.float32).astype(jnp.bfloat16)

    def reaches(last, doc):
        return (last >= 0) & (doc_of(lengths_ref, last) == doc)

    pair = lax.div(index, 2)
    joined = reaches((2 * pair + 1) * total - 1, doc_of(lengths_ref, (2 * pair + 2) * total - 1))
    flags = [odd | joined, jnp.logical_not(odd) | joined, odd & reaches(index * total - 1, first_doc)]
    for k in range(1, hops + 1):
        sender = source(pair, k)
        flags.append((sender < pair) & reaches((sender + 1) * 2 * total - 1, first_doc))
    row = lax.broadcasted_iota(jnp.int32, flags_ref.shape, 0)
    found = jnp.zeros(flags_ref.shape, jnp.int32)
    for i, flag in enumerate(flags):
        found = found + jnp.where(row == i, flag.astype(jnp.int32), 0)
    flags_ref[...] = found.astype(jnp.float32)


def project_kernel(parts, groups, before, first, weight_ref, *refs):
    rows, keep = refs[:parts], refs[parts : parts + groups]
    out_ref, state_ref = refs[parts + groups + before :]
    head = keep[0].shape[1]
    found = jnp.dot(
        jnp.concatenate([r[...] for r in rows], axis=0),
        weight_ref[:, first:],
        preferred_element_type=jnp.float32,
    ).astype(jnp.bfloat16)
    out_ref[...] = found
    kept = jnp.concatenate([r[...] for r in keep], axis=0)
    keys, values = found[:, -2 * head : -head] * kept, found[:, -head:]
    state = lax.dot_general(
        keys, values, (((0,), (0,)), ((), ())), preferred_element_type=jnp.float32
    )
    if before:
        state = state + refs[parts + groups][...]
    state_ref[...] = state.astype(state_ref.dtype)


def local_kernel(groups, weight_ref, late_kv_ref, allowed_ref, *refs):
    rows, parts, query_ref, out_ref = refs[:groups], refs[groups:-2], refs[-2], refs[-1]
    head = weight_ref.shape[1] // 3
    late = jnp.dot(
        jnp.concatenate([r[...] for r in rows], axis=0),
        weight_ref[:, :head],
        preferred_element_type=jnp.float32,
    ).astype(jnp.bfloat16)
    queries = jnp.concatenate([r[:, :head] for r in parts] + [late], axis=0)
    query_ref[...] = queries
    keys = jnp.concatenate([r[:, head : 2 * head] for r in parts] + [late_kv_ref[:, :head]], axis=0)
    values = jnp.concatenate([r[:, 2 * head :] for r in parts] + [late_kv_ref[:, head:]], axis=0)
    scores = lax.dot_general(
        queries, keys, (((1,), (1,)), ((), ())), preferred_element_type=jnp.float32
    )
    scores = scores.astype(jnp.bfloat16) * allowed_ref[...]
    out_ref[...] = jnp.dot(scores, values, preferred_element_type=jnp.float32)


def pair_kernel(flags_ref, own_ref, other_ref, out_ref):
    out_ref[...] = (
        own_ref[...].astype(jnp.float32) * flags_ref[0:1, :]
        + other_ref[...].astype(jnp.float32) * flags_ref[1:2, :]
    ).astype(out_ref.dtype)


def finish_kernel(order, flags_ref, query_ref, local_ref, takes_ref, gain_ref, *refs):
    state_refs, outs = refs[: len(order)], refs[len(order) :]
    state = jnp.zeros(state_refs[0].shape, jnp.float32)
    for k, ref in zip(order, state_refs):
        state = state + ref[...].astype(jnp.float32) * flags_ref[2 + k : 3 + k, :]
    high = state.astype(jnp.bfloat16)
    low = (state - high.astype(jnp.float32)).astype(jnp.bfloat16)
    queries = query_ref[...]
    incoming = jnp.dot(queries, high, preferred_element_type=jnp.float32) + jnp.dot(
        queries, low, preferred_element_type=jnp.float32
    )
    attended = local_ref[...] + incoming * takes_ref[...]
    inverse_rms = lax.rsqrt(jnp.mean(attended * attended, axis=1, keepdims=True) + EPSILON)
    hidden = (attended * inverse_rms * gain_ref[...]).astype(jnp.bfloat16)
    each = hidden.shape[0] // len(outs)
    for j, out_ref in enumerate(outs):
        out_ref[...] = hidden[j * each : (j + 1) * each]


def columns_of(place, piece):
    if place == 2:
        return slice(2 * piece, None)
    start = jnp.bitwise_xor(lax.rem(lax.axis_index("seq"), 2), place) * piece
    return pl.ds(pl.multiple_of(start, 128), piece)


def halve_kernel(rows_ref, first_ref, second_ref):
    half = first_ref.shape[0]
    first_ref[...] = rows_ref[:half]
    second_ref[...] = rows_ref[half:]


def cut_kernel(weight_ref, shared_ref, rest_ref):
    piece = shared_ref.shape[1]
    shared_ref[...] = weight_ref[:, columns_of(0, piece)]
    rest_ref[...] = weight_ref[:, columns_of(2, piece)]


def chip_kernel(places, piece, near_ref, far_ref, near_weight_ref, *refs):
    weights, (own_ref, other_ref) = refs[:-2], refs[-2:]
    rows = own_ref.shape[0]
    hidden = jnp.concatenate([near_ref[...], far_ref[...]], axis=1)
    done = 0
    for place, weight_ref in zip(places, weights):
        width = weight_ref.shape[1]
        weight = jnp.concatenate(
            [near_weight_ref[:, columns_of(place, piece)], weight_ref[...]], axis=0
        )
        result = jnp.dot(hidden, weight, preferred_element_type=jnp.float32)
        own_ref[:, done : done + width] = result[:rows]
        other_ref[:, done : done + width] = result[rows:].astype(other_ref.dtype)
        done += width


def sum_kernel(places, piece, *refs):
    parts, out_ref, held, sems = refs[:-3], refs[-3], refs[-2], refs[-1]
    copies, at = [], 0
    for each, own_ref, other_ref in zip(places, parts[::2], parts[1::2]):
        done = 0
        for place in each:
            width = held.shape[1] - 2 * piece if place == 2 else piece
            here, there = slice(done, done + width), slice(at, at + width)
            held[:, there] = (
                own_ref[:, here] + other_ref[:, here].astype(jnp.float32)
            ).astype(held.dtype)
            target = out_ref.at[:, columns_of(place, piece)]
            copies.append(pltpu.make_async_copy(held.at[:, there], target, sems.at[len(copies)]))
            copies[-1].start()
            done, at = done + width, at + width
    for copy in copies:
        copy.wait()


def out_kernel(hidden_ref, weight_ref, out_ref):
    out_ref[...] = jnp.dot(
        hidden_ref[...], weight_ref[...], preferred_element_type=jnp.float32
    ).astype(out_ref.dtype)


def call(kernel, out_shape, flops, *args, scalars=False):
    several = isinstance(out_shape, (list, tuple))
    return pl.pallas_call(
        kernel,
        out_shape=out_shape,
        in_specs=[SMEM if scalars and i == 0 else VMEM for i in range(len(args))],
        out_specs=[VMEM] * len(out_shape) if several else VMEM,
        cost_estimate=pl.CostEstimate(
            flops=flops,
            bytes_accessed=sum(a.size * a.dtype.itemsize for a in args) if flops else 0,
            transcendentals=0,
        ),
        compiler_params=pltpu.CompilerParams(vmem_limit_bytes=4 << 20),
    )(*args)


def swap(x, axis, bits):
    return lax.ppermute(x, axis, [(i, i ^ bits) for i in range(lax.axis_size(axis))])


def after(x, *others):
    return lax.optimization_barrier((x, *others))[0]


def body(tokens, qkv_weight, out_weight, norm_gain, doc_lengths):
    tp, seq = lax.axis_size("tp"), lax.axis_size("seq")
    head = qkv_weight.shape[1] // 3
    mine, width = tokens.shape[0], out_weight.shape[1]
    total = mine * tp
    bf16, f32 = jnp.bfloat16, jnp.float32
    shape = jax.ShapeDtypeStruct
    square = shape((head, head), bf16)
    split = tp == 4 and seq % 2 == 0
    groups = 4 if split else 1
    rows = total // groups
    piece = 5 * width // 16

    reach = -(-(MOST - 1) // total)
    hops = min(seq // 2 - 1, -(-reach // 2))
    everyone = seq == 8 and hops == 3
    *keep, takes, allowed, flags = call(
        functools.partial(mask_kernel, hops, jnp.bitwise_xor if everyone else jnp.subtract),
        [shape((rows, head), bf16)] * groups
        + [shape((total, head), f32), shape((total, total), bf16), shape((8, head), f32)],
        total * total,
        doc_lengths,
        scalars=True,
    )

    def project(x, group, *before, first=0, state_type=f32):
        found = sum(part.shape[0] for part in x)
        kept = keep[group : group + found // rows]
        return call(
            functools.partial(project_kernel, len(x), len(kept), len(before), first),
            [shape((found, 3 * head - first), bf16), shape((head, head), state_type)],
            6 * found * tokens.shape[1] * head,
            qkv_weight,
            *x,
            *kept,
            *before,
        )

    if split:
        across = swap(tokens, "tp", 2)
        own, state = project([tokens], 0)
        halves = call(halve_kernel, [shape((mine // 2, tokens.shape[1]), bf16)] * 2, 0, tokens)
        beside, state = project([swap(half, "tp", 1) for half in halves], 1, state)
        shared, rest = call(
            cut_kernel,
            [shape((head, piece), bf16), shape((head, width - 2 * piece), bf16)],
            head * width,
            out_weight,
        )
        across, own, beside, state, shared, rest, takes, allowed, flags, *keep = (
            lax.optimization_barrier(
                (across, own, beside, state, shared, rest, takes, allowed, flags, *keep)
            )
        )
        late = [across, swap(across, "tp", 1)]
        shared = swap(shared, "tp", 2)
        parts, before = [own, beside], [state]
    else:
        late = [lax.all_gather(tokens, "tp", axis=0, tiled=True)]
        parts, before = [], []
    late_kv, tail = project(late, len(parts), *before, first=head, state_type=bf16)
    other = swap(tail, "seq", 1)
    queries, local = call(
        functools.partial(local_kernel, len(late)),
        [shape((total, head), bf16), shape((total, head), f32)],
        4 * total * total * head + 2 * len(late) * late[0].size * head,
        qkv_weight,
        late_kv,
        allowed,
        *late,
        *parts,
    )
    other = after(other, local)
    pair = call(pair_kernel, square, SHORT, flags, tail, other)
    if everyone:
        pairs = [swap(pair, "seq", 2 * k) for k in range(1, hops + 1)]
    else:
        pairs = [
            lax.ppermute(pair, "seq", [(i, (i + 2 * k) % seq) for i in range(seq)])
            for k in range(1, hops + 1)
        ]
    if split:
        rest = swap(after(rest, local), "tp", 2)
        shared_other = swap(after(shared, pair), "seq", 1)
    order = (0, 1, 2, 3) if everyone else tuple(range(hops + 1))
    hidden = call(
        functools.partial(finish_kernel, order),
        [shape((total // 2, head), bf16)] * 2 if split else [shape((total, head), bf16)],
        LONG,
        flags,
        queries,
        local,
        takes,
        norm_gain.reshape(1, head),
        *[([other] + pairs)[k] for k in order],
    )
    out = shape((mine, width), bf16)
    if not split:
        mixed = lax.all_to_all(hidden[0].reshape(tp, -1, head), "tp", 0, 0, tiled=True)
        mixed = mixed.transpose(1, 0, 2).reshape(-1, tp * head)
        weight = lax.all_gather(out_weight, "tp", axis=0, tiled=True)
        tile = width // 4
        return pl.pallas_call(
            out_kernel,
            out_shape=out,
            grid=(width // tile,),
            in_specs=[
                pl.BlockSpec(mixed.shape, lambda i: (0, 0)),
                pl.BlockSpec((weight.shape[0], tile), lambda i: (0, i)),
            ],
            out_specs=pl.BlockSpec((mine, tile), lambda i: (0, i)),
        )(mixed, weight)
    near, far = hidden
    far = swap(far, "tp", 2)
    sums, places = [], ((0, 2), (1,))
    for each, pieces in zip(places, ((shared, rest), (shared_other,))):
        columns = sum(w.shape[1] for w in pieces)
        own, beside = call(
            functools.partial(chip_kernel, each, piece),
            [shape((mine, columns), f32), shape((mine, columns), bf16)],
            8 * mine * head * columns,
            near,
            far,
            out_weight,
            *pieces,
        )
        sums += [own, swap(beside, "tp", 1)]
    return pl.pallas_call(
        functools.partial(sum_kernel, places, piece),
        out_shape=out,
        in_specs=[VMEM] * len(sums),
        out_specs=pl.BlockSpec(memory_space=pltpu.HBM),
        scratch_shapes=[pltpu.VMEM((mine, width), bf16), pltpu.SemaphoreType.DMA((3,))],
        cost_estimate=pl.CostEstimate(
            flops=mine * width, bytes_accessed=7 * mine * width, transcendentals=0
        ),
        compiler_params=pltpu.CompilerParams(vmem_limit_bytes=4 << 20),
    )(*sums)


def solution(mesh):
    in_specs = (P(("seq", "tp"), None), P(None, "tp"), P("tp", None), P("tp"), P())
    out_specs = P(("seq", "tp"), None)
    return jax.shard_map(body, mesh=mesh, in_specs=in_specs, out_specs=out_specs, check_vma=False)
```
